32 devices in a mesh: win: 2 (over x), row: 16 (over z, y, core).
Axes of the slice: x: 2, y: 2, z: 4, core: 2. Of those that a mesh axis runs over, the one named last changes fastest.
Arguments:
- mask_field: float32 [2, 4096, 128], P(None, ('win', 'row')), parts along dimension 1, may hold values from -6 to 6
- target: int32 [4096, 128], P(('win', 'row')), parts along dimension 0, may hold values 0 or 1
- kernel_taps: float32 [24, 2, 128, 128], replicated, may hold values from -0.046875 to 0.046875
- kernel_radii: int32 [24], replicated, may hold values from 16 to 64, as said below
- kernel_group: int32 [24], replicated, may hold values from 0 to 2, as said below
- kernel_weight: float32 [24], replicated, may hold values from 0.1 to 1
Outputs:
- resist: float32 [3, 4096, 128], P(None, ('win', 'row')), parts along dimension 1
- gradient: float32 [2, 4096, 128], P(None, ('win', 'row')), parts along dimension 1
The draws below stay inside these ranges and needn't reach their ends.
There are 2 independent parts, one for each index of `win`. The reference program is written for one: setup_inputs(seed, part) draws one part's arguments, and reference() takes and returns one part's arrays. A program takes and returns all parts, laid end to end along the dimension named above; an argument that names none is the same for every part. Nothing has to cross between parts.
Inputs may be any that keep to these rules, and one draw needn't show every extreme that they name: `kernel_radii`: every radius lies in 16 to 64; some kernel has radius exactly 64 and some exactly 16. `kernel_group`: every one of the 3 process conditions holds at least one kernel.
All inputs are finite; a program needn't handle non-finite values. No bound on the sum of `target` on one device may be relied on, other than what follows from the above.
Results may differ from the reference program's by a relative error of at most 0.0003.
Values sent between devices are 32-bit elements; how exact they have to be, the bound alone decides.
A program may use at most 128 MiB of HBM per device.

```python
import math
import jax
import jax.numpy as jnp
from jax import lax

COLS = 128
RMAX = 64
RMIN = 16
KERNELS = 24
GROUPS = 3
ROWS = 2048


def draw_kernel_radii(key, part):
    key = jax.random.fold_in(key, 11)
    first_key, second_key = jax.random.split(key)
    values = jax.random.randint(first_key, (KERNELS,), RMIN, RMAX + 1)
    order = jax.random.permutation(second_key, KERNELS)
    values = values.at[order[0]].set(RMAX)
    values = values.at[order[1]].set(RMIN)
    return values.astype(jnp.int32)


def draw_kernel_group(key, part):
    key = jax.random.fold_in(key, 23)
    first_key, second_key = jax.random.split(key)
    values = jax.random.randint(first_key, (KERNELS,), 0, GROUPS)
    order = jax.random.permutation(second_key, KERNELS)
    values = values.at[order[:GROUPS]].set(jnp.arange(GROUPS, dtype=jnp.int32))
    return values.astype(jnp.int32)


def with_ends(result, rng, smallest, top_value):
    longest = result.shape.index(max(result.shape))
    spots = []
    for shift in (0, 1):
        where = [jax.random.randint(jax.random.fold_in(rng, axis), (), 0, length) for axis, length in enumerate(result.shape)]
        where[longest] = (where[longest] + shift) % result.shape[longest]
        spots.append(tuple(where))
    return result.at[spots[0]].set(smallest).at[spots[1]].set(top_value)


def levels(rng, extent, shards, least, high):
    level, own = 1.0, jax.random.fold_in(rng, 6)
    for axis_at, shards_of in shards:
        steps = jnp.exp(jax.random.uniform(jax.random.fold_in(own, axis_at), (shards_of,), jnp.float32, least / len(shards), high / len(shards)))
        level = level * jnp.repeat(steps, extent[axis_at] // shards_of).reshape([-1 if axis == axis_at else 1 for axis in range(len(extent))])
    return level


def normal_values(key, shape, spread, bound, pieces=(), held_as=jnp.bfloat16):
    loudness = levels(key, shape, pieces, -0.22, 0.18) if pieces else 1.0
    drawn = jax.random.normal(key, shape, jnp.float32) * spread * loudness
    return jnp.minimum(jnp.maximum(drawn, -bound), bound).astype(held_as)


def setup_inputs(seed: int = 0, part: int = 0) -> dict:
    key_of = jax.random.split(jax.random.key(seed), 7)
    part_splits = jax.random.split(jax.random.fold_in(key_of[6], part), 7)
    mask_field = normal_values(part_splits[0], (2, ROWS, COLS), 1.0, 6.0, ((1, 16),), jnp.float32)
    target = with_ends((jax.random.randint(part_splits[1], (ROWS, COLS), 0, 2) < 1).astype(jnp.int32), jax.random.fold_in(part_splits[1], 1), 0, 1)
    kernel_taps = normal_values(key_of[2], (KERNELS, 2, 2 * RMAX, 2 * RMAX), (4 * RMAX * RMAX) ** -0.5, 0.046875, (), jnp.float32)
    kernel_radii = draw_kernel_radii(jax.random.fold_in(key_of[6], 71), part)
    kernel_group = draw_kernel_group(jax.random.fold_in(key_of[6], 71), part)
    kernel_weight = jnp.clip(jnp.exp(jax.random.uniform(key_of[5], (KERNELS,), jnp.float32, math.log(0.1), math.log(1.0))), 0.1, 1.0)
    return {"mask_field": mask_field, "target": target, "kernel_taps": kernel_taps, "kernel_radii": kernel_radii, "kernel_group": kernel_group, "kernel_weight": kernel_weight}


steepness = 1.0
threshold = 2.0

def kernel_spectrum(tap_real, tap_imag, radius, grid_rows, grid_cols):
    offsets = jnp.arange(2 * RMAX, dtype=jnp.int32) - RMAX
    inside = ((offsets >= -radius) & (offsets < radius)).astype(jnp.float32)
    kept_taps = inside[:, None] * inside[None, :]
    complex_taps = lax.complex(tap_real * kept_taps, tap_imag * kept_taps)
    placed = jnp.pad(complex_taps, ((0, grid_rows - 2 * RMAX), (0, grid_cols - 2 * RMAX)))
    placed = jnp.roll(placed, (-RMAX, -RMAX), axis=(0, 1))
    return jnp.fft.fft2(placed)

def convolve(mask_real, mask_imag, spectrum):
    total_rows = mask_real.shape[0]
    total_cols = mask_real.shape[1]
    grid = jnp.pad(lax.complex(mask_real, mask_imag), ((0, 2 * RMAX), (0, 2 * RMAX)))
    result_field = jnp.fft.ifft2(jnp.fft.fft2(grid) * spectrum)[:total_rows, :total_cols]
    return (jnp.real(result_field), jnp.imag(result_field))

def reference(mask_field, target, kernel_taps, kernel_radii, kernel_group, kernel_weight):
    total_rows = mask_field.shape[1]
    total_cols = mask_field.shape[2]
    grid_rows = total_rows + 2 * RMAX
    grid_cols = total_cols + 2 * RMAX
    onehot = (kernel_group[:, None] == jnp.arange(GROUPS, dtype=jnp.int32)[None, :]).astype(jnp.float32)
    mixing = kernel_weight[:, None] * onehot
    indices = jnp.arange(KERNELS, dtype=jnp.int32)

    def spectrum_of(index):
        return kernel_spectrum(kernel_taps[index, 0], kernel_taps[index, 1], kernel_radii[index], grid_rows, grid_cols)

    def forward_step(carry, index):
        field_real, field_imag = convolve(mask_field[0], mask_field[1], spectrum_of(index))
        power = field_real * field_real + field_imag * field_imag
        return (carry + mixing[index][:, None, None] * power[None], None)
    intensity, _ = lax.scan(forward_step, jnp.zeros((GROUPS, total_rows, total_cols), jnp.float32), indices)
    resist = jax.nn.sigmoid(steepness * (intensity - threshold))
    slopes = 2.0 * (resist - target.astype(jnp.float32)[None]) * resist * (1.0 - resist) * steepness

    def adjoint_step(carry, index):
        spectrum = spectrum_of(index)

        def linear(first_part, second_part):
            return convolve(first_part, second_part, spectrum)
        (field_real, field_imag), pullback = jax.vjp(linear, mask_field[0], mask_field[1])
        factor = 2.0 * lax.optimization_barrier(jnp.sum(mixing[index][:, None, None] * slopes, axis=0))
        grad_real, grad_imag = pullback((factor * field_real, factor * field_imag))
        return (carry + jnp.stack([grad_real, grad_imag]), None)
    gradient, _ = lax.scan(adjoint_step, jnp.zeros((2, total_rows, total_cols), jnp.float32), indices)
    return (resist, gradient)
```

```python
import numpy as np

import jax
import jax.numpy as jnp
from jax import lax
from jax.experimental import pallas as pl
from jax.experimental.pallas import tpu as pltpu
from jax.sharding import PartitionSpec as P

RMAX = 64
GROUPS = 3
STEEPNESS = 1.0
THRESHOLD = 2.0
UNROLL = (4, 6, 6)
TABLES = 11
MESH = pl.DeviceIdType.MESH


def split_np(table):
    high = table.astype(jnp.bfloat16)
    low = (table - high.astype(np.float64)).astype(jnp.bfloat16)
    return high, low


def angles(twice, grid):
    freqs = np.arange(grid // 2, dtype=np.int64)
    turns = (twice.astype(np.int64)[:, None] * (2 * freqs[None, :] + 1)) % (4 * grid)
    return turns.astype(np.float64) * (np.pi / (2 * grid))


def halves(count):
    return 2 * np.arange(count // 2) + 1


def tables(rows, cols):
    taps = 2 * RMAX
    grid_rows, grid_cols = rows + taps, cols + taps
    tap, col = 2 * (np.arange(taps) - RMAX), 2 * (np.arange(cols) - RMAX)
    ext = 2 * (np.arange(grid_rows) - RMAX - rows // 2)

    def right(points, grid):
        ang = angles(points, grid)
        high, low = split_np(np.concatenate([np.cos(ang), np.sin(ang)], 1))
        return np.concatenate([high, high, low, low], 0)

    def folded(points, grid, wave):
        high, low = split_np(wave(angles(points, grid).T))
        return np.concatenate([high, high, low, low], 1)

    def left(points, grid):
        ang = angles(points, grid).T
        return np.concatenate(split_np(np.concatenate([np.cos(ang), np.sin(ang)], 0)), 0)

    def back_folded(points, grid, wave):
        high, low = split_np(wave(angles(points, grid)) / grid)
        return np.concatenate(
            [np.concatenate([high, high], 1), np.concatenate([low, low], 1)], 0
        )

    def back_left(points, grid):
        ang = angles(points, grid)
        return np.concatenate(
            split_np(np.concatenate([np.cos(ang), np.sin(ang)], 1) / grid), 0
        )

    def back_right(points, grid):
        ang = angles(points, grid).T
        high, low = split_np(np.concatenate([np.cos(ang), np.sin(ang)], 0) / grid)
        both = np.concatenate([high, low], 1)
        return np.concatenate([both, both], 0)

    return (
        right(tap, grid_cols),
        folded(halves(taps), grid_rows, np.cos),
        folded(halves(taps), grid_rows, np.sin),
        right(col, grid_cols),
        left(ext, grid_rows),
        back_folded(halves(rows), grid_rows, np.cos),
        back_folded(halves(rows), grid_rows, np.sin),
        back_right(col, grid_cols),
        folded(halves(rows), grid_rows, np.cos),
        folded(halves(rows), grid_rows, np.sin),
        back_left(ext, grid_rows),
    )


def resist_of(intensity):
    return jax.nn.sigmoid(STEEPNESS * (intensity - THRESHOLD))


def dot(a, b):
    return lax.dot_general(a, b, (((1,), (0,)), ((), ())), preferred_element_type=jnp.float32)


def split(value):
    high = value.astype(jnp.bfloat16)
    low = (value - high.astype(jnp.float32)).astype(jnp.bfloat16)
    return high, low


def fold(value):
    half = value.shape[0] // 2
    return value[:half] + value[half:]


def flip(value):
    tiles = value.reshape(value.shape[0] // 8, 8, value.shape[1])
    spot = lax.broadcasted_iota(jnp.int32, tiles.shape, 1)
    for step in (4, 2, 1):
        down = pltpu.roll(tiles, step, 1)
        up = down if step == 4 else pltpu.roll(tiles, 8 - step, 1)
        tiles = down if step == 4 else jnp.where((spot & step) == 0, up, down)
    return jnp.concatenate([tiles[i] for i in range(tiles.shape[0] - 1, -1, -1)], axis=0)


def fold_rows(plus_real, minus_real, plus_imag, minus_imag):
    return jnp.concatenate(
        [
            plus_real + minus_real,
            plus_real - minus_real,
            plus_imag + minus_imag,
            plus_imag - minus_imag,
        ],
        axis=0,
    )


def col_transform(rows, table):
    high, low = split(rows)
    return dot(jnp.concatenate([high, low, high, low], axis=1), table)


def signed(real, imag):
    width = real.shape[1] // 2
    rc, rs, ic, js = real[:, :width], real[:, width:], imag[:, :width], imag[:, width:]
    return jnp.concatenate([rc + js, ic - rs, rc - js, ic + rs], axis=1)


def unsigned(value):
    width = value.shape[1] // 4
    pr, pi, mr, mi = (value[:, i * width : (i + 1) * width] for i in range(4))
    return (
        jnp.concatenate([pr + mr, mi - pi], axis=1),
        jnp.concatenate([pi + mi, pr - mr], axis=1),
    )


def quadrants(cos_part, sin_part):
    width = cos_part.shape[1] // 4
    quads = []
    for s in range(2):
        real, imag = slice(2 * s * width, (2 * s + 1) * width), slice((2 * s + 1) * width, (2 * s + 2) * width)
        cr, ci, sr, si = cos_part[:, real], cos_part[:, imag], sin_part[:, real], sin_part[:, imag]
        quads.append((cr + si, ci - sr))
        quads.append((cr - si, ci + sr))
    return quads


def waves(quads):
    (ar, ai), (br, bi), (cr, ci), (dr, di) = quads
    cos_part = jnp.concatenate([ar + br, ai + bi, cr + dr, ci + di], axis=1)
    sin_part = jnp.concatenate([bi - ai, ar - br, di - ci, cr - dr], axis=1)
    return cos_part, sin_part


def transform(rows, col_table, cos_table, sin_table):
    half = col_transform(rows, col_table)
    quarter = half.shape[0] // 4
    er, orr, ei, oi = (half[i * quarter : (i + 1) * quarter] for i in range(4))

    def along_rows(table, value):
        high, low = split(value)
        return dot(table, jnp.concatenate([high, low, high, low], axis=0))

    return quadrants(
        along_rows(cos_table, signed(er, ei)), along_rows(sin_table, signed(orr, oi))
    )


def col_inverse(rows, table):
    high, low = split(rows)
    both = dot(jnp.concatenate([high, low], axis=1), table)
    width = both.shape[1] // 2
    return both[:, :width] + both[:, width:]


def row_transform_wide(value, table):
    high, low = split(value)
    return fold(dot(table, high)) + dot(table[: table.shape[0] // 2], low)


def inverse_folded(quads, cos_table, sin_table, col_table):
    cos_part, sin_part = waves(quads)

    def along_rows(table, value):
        high, low = split(value)
        return fold(dot(table, jnp.concatenate([high, low], axis=0)))

    er, ei = unsigned(along_rows(cos_table, cos_part))
    orr, oi = unsigned(along_rows(sin_table, sin_part))
    out = col_inverse(jnp.concatenate([er, orr, ei, oi], axis=0), col_table)
    quarter = out.shape[0] // 4
    er, orr, ei, oi = (out[i * quarter : (i + 1) * quarter] for i in range(4))
    return jnp.concatenate([er + orr, er - orr, ei + oi, ei - oi], axis=0)


def inverse_wide(quads, row_table, col_table):
    cos_part, sin_part = waves(quads)
    half = row_transform_wide(jnp.concatenate([cos_part, sin_part], axis=0), row_table)
    return col_inverse(jnp.concatenate(unsigned(half), axis=0), col_table)


def body(
    radii_ref,
    group_ref,
    weight_ref,
    taps_hbm,
    mask_hbm,
    target_hbm,
    *refs,
):
    table_hbm, refs = refs[:TABLES], refs[TABLES:]
    out_ref, own_ref, rim_ref = refs[:3]
    spec, fields, acc, power_ref, slopes, taps_ref, ext_ref, target_ref, adj, rims = refs[3:13]
    table_ref, refs = refs[13 : 13 + TABLES], refs[13 + TABLES :]
    tap_sem, load_sem, send_sem, recv_sem = refs
    tap_col, tap_cos, tap_sin, own_col, ext_row = table_ref[:5]
    back_cos, back_sin, back_col, own_cos, own_sin, back_ext = table_ref[5:]
    kernels, _, taps, _ = taps_hbm.shape
    rows, cols = target_hbm.shape
    me, count = lax.axis_index("row"), lax.axis_size("row")
    has_prev, has_next = me > 0, me < count - 1
    prev_id = {"row": lax.rem(me + count - 1, count)}
    next_id = {"row": lax.rem(me + 1, count)}

    def load(src, dst, slot):
        return pltpu.make_async_copy(src, dst, load_sem.at[slot])

    def tap_load(k):
        return pltpu.make_async_copy(taps_hbm.at[k], taps_ref.at[k], tap_sem.at[k])

    loads = [load(src, dst, i) for i, (src, dst) in enumerate(zip(table_hbm, table_ref))]
    load_mask = load(mask_hbm, ext_ref.at[:, pl.ds(RMAX, rows)], TABLES)
    load_target = load(target_hbm, target_ref, TABLES + 1)
    for i in range(3):
        loads[i].start()

    def start_tap(k, carry):
        tap_load(k).start()
        return carry

    lax.fori_loop(0, kernels, start_tap, 0)
    load_mask.start()
    load_target.start()
    for i in range(3, TABLES):
        loads[i].start()

    barrier = pltpu.get_barrier_semaphore()

    @pl.when(has_prev)
    def _():
        pl.semaphore_signal(barrier, inc=1, device_id=prev_id, device_id_type=MESH)

    @pl.when(has_next)
    def _():
        pl.semaphore_signal(barrier, inc=1, device_id=next_id, device_id_type=MESH)

    pl.semaphore_wait(barrier, has_prev.astype(jnp.int32) + has_next.astype(jnp.int32))

    def exchange(first, src_up, dst_up, src_down, dst_down):
        down = pltpu.make_async_remote_copy(
            src_ref=src_down,
            dst_ref=dst_down,
            send_sem=send_sem.at[first],
            recv_sem=recv_sem.at[first],
            device_id=next_id,
            device_id_type=MESH,
        )
        up = pltpu.make_async_remote_copy(
            src_ref=src_up,
            dst_ref=dst_up,
            send_sem=send_sem.at[first + 1],
            recv_sem=recv_sem.at[first + 1],
            device_id=prev_id,
            device_id_type=MESH,
        )
        return up, down

    def start_both(pair):
        up, down = pair

        @pl.when(has_next)
        def _():
            down.start()

        @pl.when(has_prev)
        def _():
            up.start()

    def wait_both(pair):
        up, down = pair

        @pl.when(has_prev)
        def _():
            up.wait_send()
            down.wait_recv()

        @pl.when(has_next)
        def _():
            down.wait_send()
            up.wait_recv()

    halo = exchange(
        0,
        mask_hbm.at[:, pl.ds(0, RMAX)],
        ext_ref.at[:, pl.ds(RMAX + rows, RMAX)],
        mask_hbm.at[:, pl.ds(rows - RMAX, RMAX)],
        ext_ref.at[:, pl.ds(0, RMAX)],
    )
    start_both(halo)

    @pl.when(jnp.logical_not(has_prev))
    def _():
        ext_ref[:, :RMAX] = jnp.zeros_like(ext_ref[:, :RMAX])
        rims[0] = jnp.zeros_like(rims[0])

    @pl.when(jnp.logical_not(has_next))
    def _():
        ext_ref[:, RMAX + rows :] = jnp.zeros_like(ext_ref[:, RMAX + rows :])
        rims[1] = jnp.zeros_like(rims[1])

    for i in range(3):
        loads[i].wait()

    def spectrum(k, carry):
        tap_load(k).wait()
        radius = radii_ref[k]
        a = lax.broadcasted_iota(jnp.int32, (RMAX, taps), 0)
        b = lax.broadcasted_iota(jnp.int32, (RMAX, taps), 1) - RMAX
        inside = (a < radius) & (b >= -radius) & (b < radius)
        parts = []
        for part in range(2):
            parts.append(jnp.where(inside, taps_ref[k, part, RMAX:], 0.0))
            parts.append(jnp.where(inside, flip(taps_ref[k, part, :RMAX]), 0.0))
        quads = transform(fold_rows(*parts), tap_col[...], tap_cos[...], tap_sin[...])
        for q, (re, im) in enumerate(quads):
            spec[k, 2 * q] = re
            spec[k, 2 * q + 1] = im
        return carry

    lax.fori_loop(0, kernels, spectrum, 0, unroll=UNROLL[0])

    load_mask.wait()
    load_target.wait()
    for i in range(3, TABLES):
        loads[i].wait()
    wait_both(halo)

    ext = ext_ref.shape[1]
    half = col_transform(jnp.concatenate([ext_ref[0], ext_ref[1]], axis=0), own_col[...])
    both = row_transform_wide(signed(half[:ext], half[ext:]), ext_row[...])
    middle = both.shape[0] // 2
    for q, (re, im) in enumerate(quadrants(both[:middle], both[middle:])):
        acc[2 * q] = re
        acc[2 * q + 1] = im

    power_ref[...] = jnp.zeros_like(power_ref)

    def mixed(k, g):
        return jnp.where(group_ref[k] == g, weight_ref[k], 0.0)

    def forward(k, carry):
        quads = []
        for q in range(4):
            xr, xi = spec[k, 2 * q], spec[k, 2 * q + 1]
            mr, mi = acc[2 * q], acc[2 * q + 1]
            quads.append((xr * mr - xi * mi, xr * mi + xi * mr))
        field = inverse_folded(quads, back_cos[...], back_sin[...], back_col[...])
        fields[k] = field
        power = field[:rows] * field[:rows] + field[rows:] * field[rows:]
        for g in range(GROUPS):
            power_ref[g] += mixed(k, g) * power
        return carry

    lax.fori_loop(0, kernels, forward, 0, unroll=UNROLL[1])

    half_rows = rows // 2
    target = target_ref[...].astype(jnp.float32)
    target = jnp.concatenate([target[half_rows:], flip(target[:half_rows])], axis=0)
    for g in range(GROUPS):
        power = power_ref[g]
        out_ref[g] = jnp.concatenate([flip(power[half_rows:]), power[:half_rows]], axis=0)
        resist = resist_of(power)
        slopes[g] = 2.0 * (resist - target) * resist * (1.0 - resist) * STEEPNESS
    acc[...] = jnp.zeros_like(acc)

    def backward(k, carry):
        factor = (2.0 * weight_ref[k]) * slopes[group_ref[k]]
        plus, minus = factor[:half_rows], factor[half_rows:]
        parts = []
        for part in range(2):
            parts.append(plus * fields[k, part * rows : part * rows + half_rows])
            parts.append(minus * fields[k, part * rows + half_rows : (part + 1) * rows])
        quads = transform(fold_rows(*parts), own_col[...], own_cos[...], own_sin[...])
        for q, (wr, wi) in enumerate(quads):
            xr, xi = spec[k, 2 * q], spec[k, 2 * q + 1]
            acc[2 * q] += xr * wr + xi * wi
            acc[2 * q + 1] += xr * wi - xi * wr
        return carry

    lax.fori_loop(0, kernels, backward, 0, unroll=UNROLL[2])
    quads = [(acc[2 * q], acc[2 * q + 1]) for q in range(4)]
    adjoint = inverse_wide(quads, back_ext[...], back_col[...])
    adj[0] = adjoint[:ext]
    adj[1] = adjoint[ext:]
    back = exchange(
        2,
        adj.at[:, pl.ds(0, RMAX)],
        rims.at[1],
        adj.at[:, pl.ds(RMAX + rows, RMAX)],
        rims.at[0],
    )
    start_both(back)
    own_ref[...] = adj[:, RMAX : RMAX + rows]
    if rows > 2 * RMAX:
        rim_ref[...] = jnp.zeros_like(rim_ref)
    wait_both(back)
    rim_ref[:, :RMAX] = rims[0]
    rim_ref[:, rows - RMAX :] = rims[1]


def finish(power_ref, own_ref, rim_ref, resist_ref, grad_ref):
    resist_ref[...] = resist_of(power_ref[...])
    grad_ref[...] = own_ref[...] + rim_ref[...]


def on_device(mask_field, target, kernel_taps, kernel_radii, kernel_group, kernel_weight):
    rows, cols = target.shape
    kernels, _, taps, _ = kernel_taps.shape
    grid_rows, grid_cols = rows + taps, cols + taps
    consts = [jnp.asarray(t) for t in tables(rows, cols)]
    vmem = pl.BlockSpec(memory_space=pltpu.VMEM)
    smem = pl.BlockSpec(memory_space=pltpu.SMEM)
    hbm = pl.BlockSpec(memory_space=pltpu.HBM)
    plane = (grid_rows // 2, grid_cols // 2)
    intensity, own, rim = pl.pallas_call(
        body,
        out_shape=(
            jax.ShapeDtypeStruct((GROUPS, rows, cols), jnp.float32),
            jax.ShapeDtypeStruct((2, rows, cols), jnp.float32),
            jax.ShapeDtypeStruct((2, rows, cols), jnp.float32),
        ),
        in_specs=[smem] * 3 + [hbm] * (3 + len(consts)),
        out_specs=(vmem, vmem, vmem),
        scratch_shapes=[
            pltpu.VMEM((kernels, 8) + plane, jnp.float32),
            pltpu.VMEM((kernels, 2 * rows, cols), jnp.float32),
            pltpu.VMEM((8,) + plane, jnp.float32),
            pltpu.VMEM((GROUPS, rows, cols), jnp.float32),
            pltpu.VMEM((GROUPS, rows, cols), jnp.float32),
            pltpu.VMEM(kernel_taps.shape, jnp.float32),
            pltpu.VMEM((2, grid_rows, cols), jnp.float32),
            pltpu.VMEM((rows, cols), jnp.int32),
            pltpu.VMEM((2, grid_rows, cols), jnp.float32),
            pltpu.VMEM((2, 2, RMAX, cols), jnp.float32),
        ]
        + [pltpu.VMEM(t.shape, t.dtype) for t in consts]
        + [
            pltpu.SemaphoreType.DMA((kernels,)),
            pltpu.SemaphoreType.DMA((TABLES + 2,)),
            pltpu.SemaphoreType.DMA((4,)),
            pltpu.SemaphoreType.DMA((4,)),
        ],
        compiler_params=pltpu.CompilerParams(
            vmem_limit_bytes=56 * 1024 * 1024, collective_id=0, has_side_effects=True
        ),
        name="litho",
    )(kernel_radii, kernel_group, kernel_weight, kernel_taps, mask_field, target, *consts)
    return pl.pallas_call(
        finish,
        out_shape=(
            jax.ShapeDtypeStruct((GROUPS, rows, cols), jnp.float32),
            jax.ShapeDtypeStruct((2, rows, cols), jnp.float32),
        ),
        in_specs=[vmem] * 3,
        out_specs=(vmem, vmem),
        name="finish",
    )(intensity, own, rim)


def solution(mesh):
    in_specs = (P(None, ("win", "row"), None), P(("win", "row"), None), P(), P(), P(), P())
    out_specs = (P(None, ("win", "row"), None), P(None, ("win", "row"), None))
    return jax.shard_map(
        on_device, mesh=mesh, in_specs=in_specs, out_specs=out_specs, check_vma=False
    )
```

```python
import numpy as np

import jax
import jax.numpy as jnp
from jax import lax
from jax.experimental import pallas as pl
from jax.experimental.pallas import tpu as pltpu
from jax.sharding import PartitionSpec as P

RMAX = 64
GROUPS = 3
STEEPNESS = 1.0
THRESHOLD = 2.0
UNROLL = (4, 6, 6)
TABLES = 13
MESH = pl.DeviceIdType.MESH


def split_np(table):
    high = table.astype(jnp.bfloat16)
    low = (table - high.astype(np.float64)).astype(jnp.bfloat16)
    return high, low


def angles(twice, grid):
    freqs = np.arange(grid // 2, dtype=np.int64)
    turns = (twice.astype(np.int64)[:, None] * (2 * freqs[None, :] + 1)) % (4 * grid)
    return turns.astype(np.float64) * (np.pi / (2 * grid))


def halves(count):
    return 2 * np.arange(count // 2) + 1


def grids(rows, cols):
    return rows + 2 * RMAX, cols + RMAX


def tables(rows, cols):
    taps = 2 * RMAX
    grid_rows, grid_cols = grids(rows, cols)
    tap, own = 2 * (np.arange(taps) - RMAX), 2 * (np.arange(rows) - rows // 2)
    ext = 2 * (np.arange(rows + taps) - RMAX - rows // 2)
    col = 2 * (np.arange(cols) - cols // 2)

    def right(points):
        ang = angles(points, grid_rows)
        high, low = split_np(np.concatenate([np.cos(ang), np.sin(ang)], 1))
        return np.concatenate([high, high, low, low], 0)

    def back_right(points):
        ang = angles(points, grid_rows).T
        high, low = split_np(np.concatenate([np.cos(ang), np.sin(ang)], 0) / grid_rows)
        both = np.concatenate([high, low], 1)
        return np.concatenate([both, both], 0)

    def folded(points, wave):
        high, low = split_np(wave(angles(points, grid_cols).T))
        return np.concatenate([high, high, low, low], 1)

    def back_folded(points, wave):
        high, low = split_np(wave(angles(points, grid_cols)) / grid_cols)
        return np.concatenate(
            [np.concatenate([high, high], 1), np.concatenate([low, low], 1)], 0
        )

    def left(points):
        ang = angles(points, grid_cols).T
        high, low = split_np(np.concatenate([np.cos(ang), np.sin(ang)], 0))
        return np.concatenate([high, high, low, low], 1)

    def back_left(points):
        ang = angles(points, grid_cols)
        high, low = split_np(np.concatenate([np.cos(ang), np.sin(ang)], 1) / grid_cols)
        return np.concatenate([high, high, low, low], 1)

    return (
        right(tap),
        folded(halves(taps), np.cos),
        folded(halves(taps), np.sin),
        right(ext),
        left(col),
        back_folded(halves(cols), np.cos),
        back_folded(halves(cols), np.sin),
        back_right(own),
        right(own),
        folded(halves(cols), np.cos),
        folded(halves(cols), np.sin),
        back_left(col),
        back_right(ext),
    )


def resist_of(intensity):
    return jax.nn.sigmoid(STEEPNESS * (intensity - THRESHOLD))


def dot(a, b):
    return lax.dot_general(a, b, (((1,), (0,)), ((), ())), preferred_element_type=jnp.float32)


def split(value):
    high = value.astype(jnp.bfloat16)
    low = (value - high.astype(jnp.float32)).astype(jnp.bfloat16)
    return high, low


def fold(value):
    half = value.shape[0] // 2
    return value[:half] + value[half:]


def flip(value):
    tiles = value.reshape(value.shape[0] // 8, 8, value.shape[1])
    spot = lax.broadcasted_iota(jnp.int32, tiles.shape, 1)
    for step in (4, 2, 1):
        down = pltpu.roll(tiles, step, 1)
        up = down if step == 4 else pltpu.roll(tiles, 8 - step, 1)
        tiles = down if step == 4 else jnp.where((spot & step) == 0, up, down)
    return jnp.concatenate([tiles[i] for i in range(tiles.shape[0] - 1, -1, -1)], axis=0)


def fold_rows(plus_real, minus_real, plus_imag, minus_imag):
    return jnp.concatenate(
        [
            plus_real + minus_real,
            plus_real - minus_real,
            plus_imag + minus_imag,
            plus_imag - minus_imag,
        ],
        axis=0,
    )


def lane_transform(rows, table):
    high, low = split(rows)
    return dot(jnp.concatenate([high, low, high, low], axis=1), table)


def signed(real, imag):
    width = real.shape[1] // 2
    rc, rs, ic, js = real[:, :width], real[:, width:], imag[:, :width], imag[:, width:]
    return jnp.concatenate([rc + js, ic - rs, rc - js, ic + rs], axis=1)


def unsigned(value):
    width = value.shape[1] // 4
    pr, pi, mr, mi = (value[:, i * width : (i + 1) * width] for i in range(4))
    return (
        jnp.concatenate([pr + mr, mi - pi], axis=1),
        jnp.concatenate([pi + mi, pr - mr], axis=1),
    )


def quadrants(cos_part, sin_part):
    width = cos_part.shape[1] // 4
    quads = []
    for s in range(2):
        real, imag = slice(2 * s * width, (2 * s + 1) * width), slice((2 * s + 1) * width, (2 * s + 2) * width)
        cr, ci, sr, si = cos_part[:, real], cos_part[:, imag], sin_part[:, real], sin_part[:, imag]
        quads.append((cr + si, ci - sr))
        quads.append((cr - si, ci + sr))
    return quads


def waves(quads):
    (ar, ai), (br, bi), (cr, ci), (dr, di) = quads
    cos_part = jnp.concatenate([ar + br, ai + bi, cr + dr, ci + di], axis=1)
    sin_part = jnp.concatenate([bi - ai, ar - br, di - ci, cr - dr], axis=1)
    return cos_part, sin_part


def transform(rows, lane_table, cos_table, sin_table):
    half = lane_transform(rows, lane_table)
    quarter = half.shape[0] // 4
    er, orr, ei, oi = (half[i * quarter : (i + 1) * quarter] for i in range(4))

    def along_columns(table, value):
        high, low = split(value)
        return dot(table, jnp.concatenate([high, low, high, low], axis=0))

    return quadrants(
        along_columns(cos_table, signed(er, ei)), along_columns(sin_table, signed(orr, oi))
    )


def lane_inverse(rows, table):
    high, low = split(rows)
    both = dot(jnp.concatenate([high, low], axis=1), table)
    width = both.shape[1] // 2
    return both[:, :width] + both[:, width:]


def wide(table, value):
    high, low = split(value)
    return dot(table, jnp.concatenate([high, low, high, low], axis=0))


def inverse_folded(quads, cos_table, sin_table, lane_table):
    cos_part, sin_part = waves(quads)

    def along_columns(table, value):
        high, low = split(value)
        return fold(dot(table, jnp.concatenate([high, low], axis=0)))

    er, ei = unsigned(along_columns(cos_table, cos_part))
    orr, oi = unsigned(along_columns(sin_table, sin_part))
    out = lane_inverse(jnp.concatenate([er, orr, ei, oi], axis=0), lane_table)
    quarter = out.shape[0] // 4
    er, orr, ei, oi = (out[i * quarter : (i + 1) * quarter] for i in range(4))
    return jnp.concatenate([er + orr, er - orr, ei + oi, ei - oi], axis=0)


def inverse_wide(quads, left_table, lane_table):
    cos_part, sin_part = waves(quads)
    half = wide(left_table, jnp.concatenate([cos_part, sin_part], axis=0))
    high, low = split(jnp.concatenate(unsigned(half), axis=0))
    both = dot(jnp.concatenate([high, low], axis=1), lane_table)
    width = both.shape[1] // 2
    return both[:, :width] + both[:, width:]


def body(
    radii_ref,
    group_ref,
    weight_ref,
    taps_hbm,
    mask_hbm,
    target_hbm,
    *refs,
):
    table_hbm, refs = refs[:TABLES], refs[TABLES:]
    out_ref, own_ref, rim_ref = refs[:3]
    spec, fields, acc, power_ref, slopes, taps_ref, ext_ref, target_ref, adj, rims = refs[3:13]
    table_ref, refs = refs[13 : 13 + TABLES], refs[13 + TABLES :]
    tap_sem, load_sem, send_sem, recv_sem = refs
    tap_lane, tap_cos, tap_sin, ext_lane, mask_left = table_ref[:5]
    back_cos, back_sin, back_own, own_lane, own_cos, own_sin = table_ref[5:11]
    back_left, back_ext = table_ref[11:]
    kernels, _, taps, _ = taps_hbm.shape
    rows, cols = target_hbm.shape
    me, count = lax.axis_index("row"), lax.axis_size("row")
    has_prev, has_next = me > 0, me < count - 1
    prev_id = {"row": lax.rem(me + count - 1, count)}
    next_id = {"row": lax.rem(me + 1, count)}

    def load(src, dst, slot):
        return pltpu.make_async_copy(src, dst, load_sem.at[slot])

    def tap_load(k):
        return pltpu.make_async_copy(taps_hbm.at[k], taps_ref.at[k], tap_sem.at[k])

    loads = [load(src, dst, i) for i, (src, dst) in enumerate(zip(table_hbm, table_ref))]
    load_mask = load(mask_hbm, ext_ref.at[:, pl.ds(RMAX, rows)], TABLES)
    load_target = load(target_hbm, target_ref, TABLES + 1)
    for i in range(3):
        loads[i].start()

    def start_tap(k, carry):
        tap_load(k).start()
        return carry

    lax.fori_loop(0, kernels, start_tap, 0)
    load_mask.start()
    load_target.start()
    for i in range(3, TABLES):
        loads[i].start()

    barrier = pltpu.get_barrier_semaphore()

    @pl.when(has_prev)
    def _():
        pl.semaphore_signal(barrier, inc=1, device_id=prev_id, device_id_type=MESH)

    @pl.when(has_next)
    def _():
        pl.semaphore_signal(barrier, inc=1, device_id=next_id, device_id_type=MESH)

    pl.semaphore_wait(barrier, has_prev.astype(jnp.int32) + has_next.astype(jnp.int32))

    def exchange(first, src_up, dst_up, src_down, dst_down):
        down = pltpu.make_async_remote_copy(
            src_ref=src_down,
            dst_ref=dst_down,
            send_sem=send_sem.at[first],
            recv_sem=recv_sem.at[first],
            device_id=next_id,
            device_id_type=MESH,
        )
        up = pltpu.make_async_remote_copy(
            src_ref=src_up,
            dst_ref=dst_up,
            send_sem=send_sem.at[first + 1],
            recv_sem=recv_sem.at[first + 1],
            device_id=prev_id,
            device_id_type=MESH,
        )
        return up, down

    def start_both(pair):
        up, down = pair

        @pl.when(has_next)
        def _():
            down.start()

        @pl.when(has_prev)
        def _():
            up.start()

    def wait_both(pair):
        up, down = pair

        @pl.when(has_prev)
        def _():
            up.wait_send()
            down.wait_recv()

        @pl.when(has_next)
        def _():
            down.wait_send()
            up.wait_recv()

    halo = exchange(
        0,
        mask_hbm.at[:, pl.ds(0, RMAX)],
        ext_ref.at[:, pl.ds(RMAX + rows, RMAX)],
        mask_hbm.at[:, pl.ds(rows - RMAX, RMAX)],
        ext_ref.at[:, pl.ds(0, RMAX)],
    )
    start_both(halo)

    @pl.when(jnp.logical_not(has_prev))
    def _():
        ext_ref[:, :RMAX] = jnp.zeros_like(ext_ref[:, :RMAX])
        rims[0] = jnp.zeros_like(rims[0])

    @pl.when(jnp.logical_not(has_next))
    def _():
        ext_ref[:, RMAX + rows :] = jnp.zeros_like(ext_ref[:, RMAX + rows :])
        rims[1] = jnp.zeros_like(rims[1])

    for i in range(3):
        loads[i].wait()

    def spectrum(k):
        radius = radii_ref[k]
        b = lax.broadcasted_iota(jnp.int32, (RMAX, taps), 0)
        a = lax.broadcasted_iota(jnp.int32, (RMAX, taps), 1) - RMAX
        inside = (b < radius) & (a >= -radius) & (a < radius)
        parts = []
        for part in range(2):
            turned = taps_ref[k, part].T
            parts.append(jnp.where(inside, turned[RMAX:], 0.0))
            parts.append(jnp.where(inside, flip(turned[:RMAX]), 0.0))
        quads = transform(fold_rows(*parts), tap_lane[...], tap_cos[...], tap_sin[...])
        for q, (re, im) in enumerate(quads):
            spec[k, 2 * q] = re
            spec[k, 2 * q + 1] = im

    def batch(step, carry):
        for i in range(UNROLL[0]):
            tap_load(step * UNROLL[0] + i).wait()
        for i in range(UNROLL[0]):
            spectrum(step * UNROLL[0] + i)
        return carry

    lax.fori_loop(0, kernels // UNROLL[0], batch, 0)

    load_mask.wait()
    load_target.wait()
    for i in range(3, TABLES):
        loads[i].wait()
    wait_both(halo)

    mask = jnp.concatenate([ext_ref[0].T, ext_ref[1].T], axis=0)
    half = lane_transform(mask, ext_lane[...])
    both = wide(mask_left[...], signed(half[:cols], half[cols:]))
    middle = both.shape[0] // 2
    for q, (re, im) in enumerate(quadrants(both[:middle], both[middle:])):
        acc[2 * q] = re
        acc[2 * q + 1] = im

    power_ref[...] = jnp.zeros_like(power_ref)

    def mixed(k, g):
        return jnp.where(group_ref[k] == g, weight_ref[k], 0.0)

    def forward(k, carry):
        quads = []
        for q in range(4):
            xr, xi = spec[k, 2 * q], spec[k, 2 * q + 1]
            mr, mi = acc[2 * q], acc[2 * q + 1]
            quads.append((xr * mr - xi * mi, xr * mi + xi * mr))
        field = inverse_folded(quads, back_cos[...], back_sin[...], back_own[...])
        fields[k] = field
        power = field[:cols] * field[:cols] + field[cols:] * field[cols:]
        for g in range(GROUPS):
            power_ref[g] += mixed(k, g) * power
        return carry

    lax.fori_loop(0, kernels, forward, 0, unroll=UNROLL[1])

    middle = cols // 2
    target = target_ref[...].astype(jnp.float32).T
    target = jnp.concatenate([target[middle:], flip(target[:middle])], axis=0)
    for g in range(GROUPS):
        power = power_ref[g]
        out_ref[g] = jnp.concatenate([flip(power[middle:]), power[:middle]], axis=0).T
        resist = resist_of(power)
        slopes[g] = 2.0 * (resist - target) * resist * (1.0 - resist) * STEEPNESS
    acc[...] = jnp.zeros_like(acc)

    def backward(k, carry):
        factor = (2.0 * weight_ref[k]) * slopes[group_ref[k]]
        plus, minus = factor[:middle], factor[middle:]
        parts = []
        for part in range(2):
            parts.append(plus * fields[k, part * cols : part * cols + middle])
            parts.append(minus * fields[k, part * cols + middle : (part + 1) * cols])
        quads = transform(fold_rows(*parts), own_lane[...], own_cos[...], own_sin[...])
        for q, (wr, wi) in enumerate(quads):
            xr, xi = spec[k, 2 * q], spec[k, 2 * q + 1]
            acc[2 * q] += xr * wr + xi * wi
            acc[2 * q + 1] += xr * wi - xi * wr
        return carry

    lax.fori_loop(0, kernels, backward, 0, unroll=UNROLL[2])
    quads = [(acc[2 * q], acc[2 * q + 1]) for q in range(4)]
    adjoint = inverse_wide(quads, back_left[...], back_ext[...])
    adj[0] = adjoint[:cols].T
    adj[1] = adjoint[cols:].T
    back = exchange(
        2,
        adj.at[:, pl.ds(0, RMAX)],
        rims.at[1],
        adj.at[:, pl.ds(RMAX + rows, RMAX)],
        rims.at[0],
    )
    start_both(back)
    own_ref[...] = adj[:, RMAX : RMAX + rows]
    if rows > 2 * RMAX:
        rim_ref[...] = jnp.zeros_like(rim_ref)
    wait_both(back)
    rim_ref[:, :RMAX] = rims[0]
    rim_ref[:, rows - RMAX :] = rims[1]


def finish(power_ref, own_ref, rim_ref, resist_ref, grad_ref):
    resist_ref[...] = resist_of(power_ref[...])
    grad_ref[...] = own_ref[...] + rim_ref[...]


def on_device(mask_field, target, kernel_taps, kernel_radii, kernel_group, kernel_weight):
    rows, cols = target.shape
    kernels, _, taps, _ = kernel_taps.shape
    grid_rows, grid_cols = grids(rows, cols)
    consts = [jnp.asarray(t) for t in tables(rows, cols)]
    vmem = pl.BlockSpec(memory_space=pltpu.VMEM)
    smem = pl.BlockSpec(memory_space=pltpu.SMEM)
    hbm = pl.BlockSpec(memory_space=pltpu.HBM)
    plane = (grid_cols // 2, grid_rows // 2)
    intensity, own, rim = pl.pallas_call(
        body,
        out_shape=(
            jax.ShapeDtypeStruct((GROUPS, rows, cols), jnp.float32),
            jax.ShapeDtypeStruct((2, rows, cols), jnp.float32),
            jax.ShapeDtypeStruct((2, rows, cols), jnp.float32),
        ),
        in_specs=[smem] * 3 + [hbm] * (3 + len(consts)),
        out_specs=(vmem, vmem, vmem),
        scratch_shapes=[
            pltpu.VMEM((kernels, 8) + plane, jnp.float32),
            pltpu.VMEM((kernels, 2 * cols, rows), jnp.float32),
            pltpu.VMEM((8,) + plane, jnp.float32),
            pltpu.VMEM((GROUPS, cols, rows), jnp.float32),
            pltpu.VMEM((GROUPS, cols, rows), jnp.float32),
            pltpu.VMEM(kernel_taps.shape, jnp.float32),
            pltpu.VMEM((2, rows + taps, cols), jnp.float32),
            pltpu.VMEM((rows, cols), jnp.int32),
            pltpu.VMEM((2, rows + taps, cols), jnp.float32),
            pltpu.VMEM((2, 2, RMAX, cols), jnp.float32),
        ]
        + [pltpu.VMEM(t.shape, t.dtype) for t in consts]
        + [
            pltpu.SemaphoreType.DMA((kernels,)),
            pltpu.SemaphoreType.DMA((TABLES + 2,)),
            pltpu.SemaphoreType.DMA((4,)),
            pltpu.SemaphoreType.DMA((4,)),
        ],
        compiler_params=pltpu.CompilerParams(
            vmem_limit_bytes=56 * 1024 * 1024, collective_id=0, has_side_effects=True
        ),
        name="litho",
    )(kernel_radii, kernel_group, kernel_weight, kernel_taps, mask_field, target, *consts)
    return pl.pallas_call(
        finish,
        out_shape=(
            jax.ShapeDtypeStruct((GROUPS, rows, cols), jnp.float32),
            jax.ShapeDtypeStruct((2, rows, cols), jnp.float32),
        ),
        in_specs=[vmem] * 3,
        out_specs=(vmem, vmem),
        name="finish",
    )(intensity, own, rim)


def solution(mesh):
    in_specs = (P(None, ("win", "row"), None), P(("win", "row"), None), P(), P(), P(), P())
    out_specs = (P(None, ("win", "row"), None), P(None, ("win", "row"), None))
    return jax.shard_map(
        on_device, mesh=mesh, in_specs=in_specs, out_specs=out_specs, check_vma=False
    )
```

```python
import numpy as np

import jax
import jax.numpy as jnp
from jax import lax
from jax.experimental import pallas as pl
from jax.experimental.pallas import tpu as pltpu
from jax.sharding import PartitionSpec as P

RMAX = 64
GROUPS = 3
STEEPNESS = 1.0
THRESHOLD = 2.0
UNROLL = (12, 12, 12)
TABLES = 13
MESH = pl.DeviceIdType.MESH


def split_np(table):
    high = table.astype(jnp.bfloat16)
    low = (table - high.astype(np.float64)).astype(jnp.bfloat16)
    return high, low


def angles(twice, grid):
    freqs = np.arange(grid // 2, dtype=np.int64)
    turns = (twice.astype(np.int64)[:, None] * (2 * freqs[None, :] + 1)) % (4 * grid)
    return turns.astype(np.float64) * (np.pi / (2 * grid))


def halves(count):
    return 2 * np.arange(count // 2) + 1


def grids(rows, cols):
    return rows + 2 * RMAX, cols + RMAX


def tables(rows, cols):
    taps = 2 * RMAX
    grid_rows, grid_cols = grids(rows, cols)
    tap, own = 2 * (np.arange(taps) - RMAX), 2 * (np.arange(rows) - rows // 2)
    ext = 2 * (np.arange(rows + taps) - RMAX - rows // 2)
    col = 2 * (np.arange(cols) - cols // 2)

    def right(points):
        ang = angles(points, grid_rows)
        high, low = split_np(np.concatenate([np.cos(ang), np.sin(ang)], 1))
        return np.concatenate([high, high, low, low], 0)

    def back_right(points):
        ang = angles(points, grid_rows).T
        high, low = split_np(np.concatenate([np.cos(ang), np.sin(ang)], 0) / grid_rows)
        both = np.concatenate([high, low], 1)
        return np.concatenate([both, both], 0)

    def folded(points, wave):
        high, low = split_np(wave(angles(points, grid_cols).T))
        return np.concatenate([high, high, low, low], 1)

    def back_folded(points, wave):
        high, low = split_np(wave(angles(points, grid_cols)) / grid_cols)
        return np.concatenate(
            [np.concatenate([high, high], 1), np.concatenate([low, low], 1)], 0
        )

    def left(points):
        ang = angles(points, grid_cols).T
        high, low = split_np(np.concatenate([np.cos(ang), np.sin(ang)], 0))
        return np.concatenate([high, high, low, low], 1)

    def back_left(points):
        ang = angles(points, grid_cols)
        high, low = split_np(np.concatenate([np.cos(ang), np.sin(ang)], 1) / grid_cols)
        return np.concatenate([high, high, low, low], 1)

    return (
        right(tap),
        folded(halves(taps), np.cos),
        folded(halves(taps), np.sin),
        right(ext),
        left(col),
        back_folded(halves(cols), np.cos),
        back_folded(halves(cols), np.sin),
        back_right(own),
        right(own),
        folded(halves(cols), np.cos),
        folded(halves(cols), np.sin),
        back_left(col),
        back_right(ext),
    )


def resist_of(intensity):
    return jax.nn.sigmoid(STEEPNESS * (intensity - THRESHOLD))


def dot(a, b):
    return lax.dot_general(a, b, (((1,), (0,)), ((), ())), preferred_element_type=jnp.float32)


def split(value):
    high = value.astype(jnp.bfloat16)
    low = (value - high.astype(jnp.float32)).astype(jnp.bfloat16)
    return high, low


def fold(value):
    half = value.shape[0] // 2
    return value[:half] + value[half:]


def flip(value):
    tiles = value.reshape(value.shape[0] // 8, 8, value.shape[1])
    spot = lax.broadcasted_iota(jnp.int32, tiles.shape, 1)
    for step in (4, 2, 1):
        down = pltpu.roll(tiles, step, 1)
        up = down if step == 4 else pltpu.roll(tiles, 8 - step, 1)
        tiles = down if step == 4 else jnp.where((spot & step) == 0, up, down)
    return jnp.concatenate([tiles[i] for i in range(tiles.shape[0] - 1, -1, -1)], axis=0)


def fold_rows(plus_real, minus_real, plus_imag, minus_imag):
    return jnp.concatenate(
        [
            plus_real + minus_real,
            plus_real - minus_real,
            plus_imag + minus_imag,
            plus_imag - minus_imag,
        ],
        axis=0,
    )


def lane_transform(rows, table):
    high, low = split(rows)
    return dot(jnp.concatenate([high, low, high, low], axis=1), table)


def signed(real, imag):
    width = real.shape[1] // 2
    rc, rs, ic, js = real[:, :width], real[:, width:], imag[:, :width], imag[:, width:]
    return jnp.concatenate([rc + js, ic - rs, rc - js, ic + rs], axis=1)


def unsigned(value):
    width = value.shape[1] // 4
    pr, pi, mr, mi = (value[:, i * width : (i + 1) * width] for i in range(4))
    return (
        jnp.concatenate([pr + mr, mi - pi], axis=1),
        jnp.concatenate([pi + mi, pr - mr], axis=1),
    )


def quadrants(cos_part, sin_part):
    width = cos_part.shape[1] // 4
    quads = []
    for s in range(2):
        real, imag = slice(2 * s * width, (2 * s + 1) * width), slice((2 * s + 1) * width, (2 * s + 2) * width)
        cr, ci, sr, si = cos_part[:, real], cos_part[:, imag], sin_part[:, real], sin_part[:, imag]
        quads.append((cr + si, ci - sr))
        quads.append((cr - si, ci + sr))
    return quads


def waves(quads):
    (ar, ai), (br, bi), (cr, ci), (dr, di) = quads
    cos_part = jnp.concatenate([ar + br, ai + bi, cr + dr, ci + di], axis=1)
    sin_part = jnp.concatenate([bi - ai, ar - br, di - ci, cr - dr], axis=1)
    return cos_part, sin_part


def transform(rows, lane_table, cos_table, sin_table):
    half = lane_transform(rows, lane_table)
    quarter = half.shape[0] // 4
    er, orr, ei, oi = (half[i * quarter : (i + 1) * quarter] for i in range(4))

    def along_columns(table, value):
        high, low = split(value)
        return dot(table, jnp.concatenate([high, low, high, low], axis=0))

    return quadrants(
        along_columns(cos_table, signed(er, ei)), along_columns(sin_table, signed(orr, oi))
    )


def lane_inverse(rows, table):
    high, low = split(rows)
    both = dot(jnp.concatenate([high, low], axis=1), table)
    width = both.shape[1] // 2
    return both[:, :width] + both[:, width:]


def wide(table, value):
    high, low = split(value)
    return dot(table, jnp.concatenate([high, low, high, low], axis=0))


def inverse_folded(quads, cos_table, sin_table, lane_table):
    cos_part, sin_part = waves(quads)

    def along_columns(table, value):
        high, low = split(value)
        return fold(dot(table, jnp.concatenate([high, low], axis=0)))

    er, ei = unsigned(along_columns(cos_table, cos_part))
    orr, oi = unsigned(along_columns(sin_table, sin_part))
    out = lane_inverse(jnp.concatenate([er, orr, ei, oi], axis=0), lane_table)
    quarter = out.shape[0] // 4
    er, orr, ei, oi = (out[i * quarter : (i + 1) * quarter] for i in range(4))
    return jnp.concatenate([er + orr, er - orr, ei + oi, ei - oi], axis=0)


def inverse_wide(quads, left_table, lane_table):
    cos_part, sin_part = waves(quads)
    half = wide(left_table, jnp.concatenate([cos_part, sin_part], axis=0))
    high, low = split(jnp.concatenate(unsigned(half), axis=0))
    both = dot(jnp.concatenate([high, low], axis=1), lane_table)
    width = both.shape[1] // 2
    return both[:, :width] + both[:, width:]


def body(
    radii_ref,
    group_ref,
    weight_ref,
    taps_hbm,
    mask_hbm,
    target_hbm,
    *refs,
):
    table_hbm, refs = refs[:TABLES], refs[TABLES:]
    out_ref, own_ref, rim_ref = refs[:3]
    spec, fields, acc, power_ref, slopes, taps_ref, ext_ref, target_ref, adj, rims = refs[3:13]
    table_ref, refs = refs[13 : 13 + TABLES], refs[13 + TABLES :]
    tap_sem, load_sem, send_sem, recv_sem = refs
    tap_lane, tap_cos, tap_sin, ext_lane, mask_left = table_ref[:5]
    back_cos, back_sin, back_own, own_lane, own_cos, own_sin = table_ref[5:11]
    back_left, back_ext = table_ref[11:]
    kernels, _, taps, _ = taps_hbm.shape
    rows, cols = target_hbm.shape
    me, count = lax.axis_index("row"), lax.axis_size("row")
    has_prev, has_next = me > 0, me < count - 1
    prev_id = {"row": lax.rem(me + count - 1, count)}
    next_id = {"row": lax.rem(me + 1, count)}

    def load(src, dst, slot):
        return pltpu.make_async_copy(src, dst, load_sem.at[slot])

    def tap_load(k):
        return pltpu.make_async_copy(taps_hbm.at[k], taps_ref.at[k], tap_sem.at[k])

    loads = [load(src, dst, i) for i, (src, dst) in enumerate(zip(table_hbm, table_ref))]
    load_mask = load(mask_hbm, ext_ref.at[:, pl.ds(RMAX, rows)], TABLES)
    load_target = load(target_hbm, target_ref, TABLES + 1)
    for i in range(3):
        loads[i].start()

    def start_tap(k, carry):
        tap_load(k).start()
        return carry

    lax.fori_loop(0, kernels, start_tap, 0)
    load_mask.start()
    load_target.start()
    for i in range(3, TABLES):
        loads[i].start()

    barrier = pltpu.get_barrier_semaphore()

    @pl.when(has_prev)
    def _():
        pl.semaphore_signal(barrier, inc=1, device_id=prev_id, device_id_type=MESH)

    @pl.when(has_next)
    def _():
        pl.semaphore_signal(barrier, inc=1, device_id=next_id, device_id_type=MESH)

    pl.semaphore_wait(barrier, has_prev.astype(jnp.int32) + has_next.astype(jnp.int32))

    def exchange(first, src_up, dst_up, src_down, dst_down):
        down = pltpu.make_async_remote_copy(
            src_ref=src_down,
            dst_ref=dst_down,
            send_sem=send_sem.at[first],
            recv_sem=recv_sem.at[first],
            device_id=next_id,
            device_id_type=MESH,
        )
        up = pltpu.make_async_remote_copy(
            src_ref=src_up,
            dst_ref=dst_up,
            send_sem=send_sem.at[first + 1],
            recv_sem=recv_sem.at[first + 1],
            device_id=prev_id,
            device_id_type=MESH,
        )
        return up, down

    def start_both(pair):
        up, down = pair

        @pl.when(has_next)
        def _():
            down.start()

        @pl.when(has_prev)
        def _():
            up.start()

    def wait_both(pair):
        up, down = pair

        @pl.when(has_prev)
        def _():
            up.wait_send()
            down.wait_recv()

        @pl.when(has_next)
        def _():
            down.wait_send()
            up.wait_recv()

    halo = exchange(
        0,
        mask_hbm.at[:, pl.ds(0, RMAX)],
        ext_ref.at[:, pl.ds(RMAX + rows, RMAX)],
        mask_hbm.at[:, pl.ds(rows - RMAX, RMAX)],
        ext_ref.at[:, pl.ds(0, RMAX)],
    )
    start_both(halo)

    @pl.when(jnp.logical_not(has_prev))
    def _():
        ext_ref[:, :RMAX] = jnp.zeros_like(ext_ref[:, :RMAX])
        rims[0] = jnp.zeros_like(rims[0])

    @pl.when(jnp.logical_not(has_next))
    def _():
        ext_ref[:, RMAX + rows :] = jnp.zeros_like(ext_ref[:, RMAX + rows :])
        rims[1] = jnp.zeros_like(rims[1])

    for i in range(3):
        loads[i].wait()

    def spectrum(k):
        radius = radii_ref[k]
        b = lax.broadcasted_iota(jnp.int32, (RMAX, taps), 0)
        a = lax.broadcasted_iota(jnp.int32, (RMAX, taps), 1) - RMAX
        inside = (b < radius) & (a >= -radius) & (a < radius)
        parts = []
        for part in range(2):
            turned = taps_ref[k, part].T
            parts.append(jnp.where(inside, turned[RMAX:], 0.0))
            parts.append(jnp.where(inside, flip(turned[:RMAX]), 0.0))
        quads = transform(fold_rows(*parts), tap_lane[...], tap_cos[...], tap_sin[...])
        for q, (re, im) in enumerate(quads):
            spec[k, 2 * q] = re
            spec[k, 2 * q + 1] = im

    def batch(step, carry):
        for i in range(UNROLL[0]):
            tap_load(step * UNROLL[0] + i).wait()
        for i in range(UNROLL[0]):
            spectrum(step * UNROLL[0] + i)
        return carry

    lax.fori_loop(0, kernels // UNROLL[0], batch, 0)

    load_mask.wait()
    load_target.wait()
    for i in range(3, TABLES):
        loads[i].wait()
    wait_both(halo)

    mask = jnp.concatenate([ext_ref[0].T, ext_ref[1].T], axis=0)
    half = lane_transform(mask, ext_lane[...])
    both = wide(mask_left[...], signed(half[:cols], half[cols:]))
    middle = both.shape[0] // 2
    for q, (re, im) in enumerate(quadrants(both[:middle], both[middle:])):
        acc[2 * q] = re
        acc[2 * q + 1] = im

    power_ref[...] = jnp.zeros_like(power_ref)

    def mixed(k, g):
        return jnp.where(group_ref[k] == g, weight_ref[k], 0.0)

    def forward(k, carry):
        quads = []
        for q in range(4):
            xr, xi = spec[k, 2 * q], spec[k, 2 * q + 1]
            mr, mi = acc[2 * q], acc[2 * q + 1]
            quads.append((xr * mr - xi * mi, xr * mi + xi * mr))
        field = inverse_folded(quads, back_cos[...], back_sin[...], back_own[...])
        fields[k] = field
        power = field[:cols] * field[:cols] + field[cols:] * field[cols:]
        for g in range(GROUPS):
            power_ref[g] += mixed(k, g) * power
        return carry

    lax.fori_loop(0, kernels, forward, 0, unroll=UNROLL[1])

    middle = cols // 2
    target = target_ref[...].astype(jnp.float32).T
    target = jnp.concatenate([target[middle:], flip(target[:middle])], axis=0)
    for g in range(GROUPS):
        power = power_ref[g]
        out_ref[g] = jnp.concatenate([flip(power[middle:]), power[:middle]], axis=0).T
        resist = resist_of(power)
        slopes[g] = 2.0 * (resist - target) * resist * (1.0 - resist) * STEEPNESS
    acc[...] = jnp.zeros_like(acc)

    def backward(k, carry):
        factor = (2.0 * weight_ref[k]) * slopes[group_ref[k]]
        plus, minus = factor[:middle], factor[middle:]
        parts = []
        for part in range(2):
            parts.append(plus * fields[k, part * cols : part * cols + middle])
            parts.append(minus * fields[k, part * cols + middle : (part + 1) * cols])
        quads = transform(fold_rows(*parts), own_lane[...], own_cos[...], own_sin[...])
        for q, (wr, wi) in enumerate(quads):
            xr, xi = spec[k, 2 * q], spec[k, 2 * q + 1]
            acc[2 * q] += xr * wr + xi * wi
            acc[2 * q + 1] += xr * wi - xi * wr
        return carry

    lax.fori_loop(0, kernels, backward, 0, unroll=UNROLL[2])
    quads = [(acc[2 * q], acc[2 * q + 1]) for q in range(4)]
    adjoint = inverse_wide(quads, back_left[...], back_ext[...])
    adj[0] = adjoint[:cols].T
    adj[1] = adjoint[cols:].T
    back = exchange(
        2,
        adj.at[:, pl.ds(0, RMAX)],
        rims.at[1],
        adj.at[:, pl.ds(RMAX + rows, RMAX)],
        rims.at[0],
    )
    start_both(back)
    own_ref[...] = adj[:, RMAX : RMAX + rows]
    if rows > 2 * RMAX:
        rim_ref[...] = jnp.zeros_like(rim_ref)
    wait_both(back)
    rim_ref[:, :RMAX] = rims[0]
    rim_ref[:, rows - RMAX :] = rims[1]


def finish(power_ref, own_ref, rim_ref, resist_ref, grad_ref):
    resist_ref[...] = resist_of(power_ref[...])
    grad_ref[...] = own_ref[...] + rim_ref[...]


def on_device(mask_field, target, kernel_taps, kernel_radii, kernel_group, kernel_weight):
    rows, cols = target.shape
    kernels, _, taps, _ = kernel_taps.shape
    grid_rows, grid_cols = grids(rows, cols)
    consts = [jnp.asarray(t) for t in tables(rows, cols)]
    vmem = pl.BlockSpec(memory_space=pltpu.VMEM)
    smem = pl.BlockSpec(memory_space=pltpu.SMEM)
    hbm = pl.BlockSpec(memory_space=pltpu.HBM)
    plane = (grid_cols // 2, grid_rows // 2)
    intensity, own, rim = pl.pallas_call(
        body,
        out_shape=(
            jax.ShapeDtypeStruct((GROUPS, rows, cols), jnp.float32),
            jax.ShapeDtypeStruct((2, rows, cols), jnp.float32),
            jax.ShapeDtypeStruct((2, rows, cols), jnp.float32),
        ),
        in_specs=[smem] * 3 + [hbm] * (3 + len(consts)),
        out_specs=(vmem, vmem, vmem),
        scratch_shapes=[
            pltpu.VMEM((kernels, 8) + plane, jnp.float32),
            pltpu.VMEM((kernels, 2 * cols, rows), jnp.float32),
            pltpu.VMEM((8,) + plane, jnp.float32),
            pltpu.VMEM((GROUPS, cols, rows), jnp.float32),
            pltpu.VMEM((GROUPS, cols, rows), jnp.float32),
            pltpu.VMEM(kernel_taps.shape, jnp.float32),
            pltpu.VMEM((2, rows + taps, cols), jnp.float32),
            pltpu.VMEM((rows, cols), jnp.int32),
            pltpu.VMEM((2, rows + taps, cols), jnp.float32),
            pltpu.VMEM((2, 2, RMAX, cols), jnp.float32),
        ]
        + [pltpu.VMEM(t.shape, t.dtype) for t in consts]
        + [
            pltpu.SemaphoreType.DMA((kernels,)),
            pltpu.SemaphoreType.DMA((TABLES + 2,)),
            pltpu.SemaphoreType.DMA((4,)),
            pltpu.SemaphoreType.DMA((4,)),
        ],
        compiler_params=pltpu.CompilerParams(
            vmem_limit_bytes=56 * 1024 * 1024, collective_id=0, has_side_effects=True
        ),
        name="litho",
    )(kernel_radii, kernel_group, kernel_weight, kernel_taps, mask_field, target, *consts)
    return pl.pallas_call(
        finish,
        out_shape=(
            jax.ShapeDtypeStruct((GROUPS, rows, cols), jnp.float32),
            jax.ShapeDtypeStruct((2, rows, cols), jnp.float32),
        ),
        in_specs=[vmem] * 3,
        out_specs=(vmem, vmem),
        name="finish",
    )(intensity, own, rim)


def solution(mesh):
    in_specs = (P(None, ("win", "row"), None), P(("win", "row"), None), P(), P(), P(), P())
    out_specs = (P(None, ("win", "row"), None), P(None, ("win", "row"), None))
    return jax.shard_map(
        on_device, mesh=mesh, in_specs=in_specs, out_specs=out_specs, check_vma=False
    )
```

```python
import numpy as np

import jax
import jax.numpy as jnp
from jax import lax
from jax.experimental import pallas as pl
from jax.experimental.pallas import tpu as pltpu
from jax.sharding import PartitionSpec as P

RMAX = 64
GROUPS = 3
STEEPNESS = 1.0
THRESHOLD = 2.0
UNROLL = (12, 24, 24)
TABLES = 13
MESH = pl.DeviceIdType.MESH


def split_np(table):
    high = table.astype(jnp.bfloat16)
    low = (table - high.astype(np.float64)).astype(jnp.bfloat16)
    return high, low


def angles(twice, grid):
    freqs = np.arange(grid // 2, dtype=np.int64)
    turns = (twice.astype(np.int64)[:, None] * (2 * freqs[None, :] + 1)) % (4 * grid)
    return turns.astype(np.float64) * (np.pi / (2 * grid))


def halves(count):
    return 2 * np.arange(count // 2) + 1


def grids(rows, cols):
    return rows + 2 * RMAX, cols + RMAX


def tables(rows, cols):
    taps = 2 * RMAX
    grid_rows, grid_cols = grids(rows, cols)
    tap, own = 2 * (np.arange(taps) - RMAX), 2 * (np.arange(rows) - rows // 2)
    ext = 2 * (np.arange(rows + taps) - RMAX - rows // 2)
    col = 2 * (np.arange(cols) - cols // 2)

    def right(points):
        ang = angles(points, grid_rows)
        high, low = split_np(np.concatenate([np.cos(ang), np.sin(ang)], 1))
        return np.concatenate([high, high, low, low], 0)

    def back_right(points):
        ang = angles(points, grid_rows).T
        high, low = split_np(np.concatenate([np.cos(ang), np.sin(ang)], 0) / grid_rows)
        both = np.concatenate([high, low], 1)
        return np.concatenate([both, both], 0)

    def folded(points, wave):
        high, low = split_np(wave(angles(points, grid_cols).T))
        return np.concatenate([high, high, low, low], 1)

    def back_folded(points, wave):
        high, low = split_np(wave(angles(points, grid_cols)) / grid_cols)
        return np.concatenate(
            [np.concatenate([high, high], 1), np.concatenate([low, low], 1)], 0
        )

    def left(points):
        ang = angles(points, grid_cols).T
        high, low = split_np(np.concatenate([np.cos(ang), np.sin(ang)], 0))
        return np.concatenate([high, high, low, low], 1)

    def back_left(points):
        ang = angles(points, grid_cols)
        high, low = split_np(np.concatenate([np.cos(ang), np.sin(ang)], 1) / grid_cols)
        return np.concatenate([high, high, low, low], 1)

    return (
        right(tap),
        folded(halves(taps), np.cos),
        folded(halves(taps), np.sin),
        right(ext),
        left(col),
        back_folded(halves(cols), np.cos),
        back_folded(halves(cols), np.sin),
        back_right(own),
        right(own),
        folded(halves(cols), np.cos),
        folded(halves(cols), np.sin),
        back_left(col),
        back_right(ext),
    )


def resist_of(intensity):
    return jax.nn.sigmoid(STEEPNESS * (intensity - THRESHOLD))


def dot(a, b):
    return lax.dot_general(a, b, (((1,), (0,)), ((), ())), preferred_element_type=jnp.float32)


def split(value):
    high = value.astype(jnp.bfloat16)
    low = (value - high.astype(jnp.float32)).astype(jnp.bfloat16)
    return high, low


def fold(value):
    half = value.shape[0] // 2
    return value[:half] + value[half:]


def flip(value):
    tiles = value.reshape(value.shape[0] // 8, 8, value.shape[1])
    spot = lax.broadcasted_iota(jnp.int32, tiles.shape, 1)
    for step in (4, 2, 1):
        down = pltpu.roll(tiles, step, 1)
        up = down if step == 4 else pltpu.roll(tiles, 8 - step, 1)
        tiles = down if step == 4 else jnp.where((spot & step) == 0, up, down)
    return jnp.concatenate([tiles[i] for i in range(tiles.shape[0] - 1, -1, -1)], axis=0)


def fold_rows(plus_real, minus_real, plus_imag, minus_imag):
    return jnp.concatenate(
        [
            plus_real + minus_real,
            plus_real - minus_real,
            plus_imag + minus_imag,
            plus_imag - minus_imag,
        ],
        axis=0,
    )


def lane_transform(rows, table):
    high, low = split(rows)
    return dot(jnp.concatenate([high, low, high, low], axis=1), table)


def signed(real, imag):
    width = real.shape[1] // 2
    rc, rs, ic, js = real[:, :width], real[:, width:], imag[:, :width], imag[:, width:]
    return jnp.concatenate([rc + js, ic - rs, rc - js, ic + rs], axis=1)


def unsigned(value):
    width = value.shape[1] // 4
    pr, pi, mr, mi = (value[:, i * width : (i + 1) * width] for i in range(4))
    return (
        jnp.concatenate([pr + mr, mi - pi], axis=1),
        jnp.concatenate([pi + mi, pr - mr], axis=1),
    )


def quadrants(cos_part, sin_part):
    width = cos_part.shape[1] // 4
    quads = []
    for s in range(2):
        real, imag = slice(2 * s * width, (2 * s + 1) * width), slice((2 * s + 1) * width, (2 * s + 2) * width)
        cr, ci, sr, si = cos_part[:, real], cos_part[:, imag], sin_part[:, real], sin_part[:, imag]
        quads.append((cr + si, ci - sr))
        quads.append((cr - si, ci + sr))
    return quads


def waves(quads):
    (ar, ai), (br, bi), (cr, ci), (dr, di) = quads
    cos_part = jnp.concatenate([ar + br, ai + bi, cr + dr, ci + di], axis=1)
    sin_part = jnp.concatenate([bi - ai, ar - br, di - ci, cr - dr], axis=1)
    return cos_part, sin_part


def transform(rows, lane_table, cos_table, sin_table):
    half = lane_transform(rows, lane_table)
    quarter = half.shape[0] // 4
    er, orr, ei, oi = (half[i * quarter : (i + 1) * quarter] for i in range(4))

    def along_columns(table, value):
        high, low = split(value)
        return dot(table, jnp.concatenate([high, low, high, low], axis=0))

    return quadrants(
        along_columns(cos_table, signed(er, ei)), along_columns(sin_table, signed(orr, oi))
    )


def lane_inverse(rows, table):
    high, low = split(rows)
    both = dot(jnp.concatenate([high, low], axis=1), table)
    width = both.shape[1] // 2
    return both[:, :width] + both[:, width:]


def wide(table, value):
    high, low = split(value)
    return dot(table, jnp.concatenate([high, low, high, low], axis=0))


def inverse_folded(quads, cos_table, sin_table, lane_table):
    cos_part, sin_part = waves(quads)

    def along_columns(table, value):
        high, low = split(value)
        return fold(dot(table, jnp.concatenate([high, low], axis=0)))

    er, ei = unsigned(along_columns(cos_table, cos_part))
    orr, oi = unsigned(along_columns(sin_table, sin_part))
    out = lane_inverse(jnp.concatenate([er, orr, ei, oi], axis=0), lane_table)
    quarter = out.shape[0] // 4
    er, orr, ei, oi = (out[i * quarter : (i + 1) * quarter] for i in range(4))
    return jnp.concatenate([er + orr, er - orr, ei + oi, ei - oi], axis=0)


def inverse_wide(quads, left_table, lane_table):
    cos_part, sin_part = waves(quads)
    half = wide(left_table, jnp.concatenate([cos_part, sin_part], axis=0))
    high, low = split(jnp.concatenate(unsigned(half), axis=0))
    both = dot(jnp.concatenate([high, low], axis=1), lane_table)
    width = both.shape[1] // 2
    return both[:, :width] + both[:, width:]


def body(
    radii_ref,
    group_ref,
    weight_ref,
    taps_hbm,
    mask_hbm,
    target_hbm,
    *refs,
):
    table_hbm, refs = refs[:TABLES], refs[TABLES:]
    out_ref, own_ref, rim_ref = refs[:3]
    spec, fields, acc, power_ref, slopes, taps_ref, ext_ref, target_ref, adj, rims = refs[3:13]
    table_ref, refs = refs[13 : 13 + TABLES], refs[13 + TABLES :]
    tap_sem, load_sem, send_sem, recv_sem = refs
    tap_lane, tap_cos, tap_sin, ext_lane, mask_left = table_ref[:5]
    back_cos, back_sin, back_own, own_lane, own_cos, own_sin = table_ref[5:11]
    back_left, back_ext = table_ref[11:]
    kernels, _, taps, _ = taps_hbm.shape
    rows, cols = target_hbm.shape
    me, count = lax.axis_index("row"), lax.axis_size("row")
    has_prev, has_next = me > 0, me < count - 1
    prev_id = {"row": lax.rem(me + count - 1, count)}
    next_id = {"row": lax.rem(me + 1, count)}

    def load(src, dst, slot):
        return pltpu.make_async_copy(src, dst, load_sem.at[slot])

    def tap_load(k):
        return pltpu.make_async_copy(taps_hbm.at[k], taps_ref.at[k], tap_sem.at[k])

    loads = [load(src, dst, i) for i, (src, dst) in enumerate(zip(table_hbm, table_ref))]
    load_mask = load(mask_hbm, ext_ref.at[:, pl.ds(RMAX, rows)], TABLES)
    load_target = load(target_hbm, target_ref, TABLES + 1)
    for i in range(3):
        loads[i].start()

    def start_tap(k, carry):
        tap_load(k).start()
        return carry

    lax.fori_loop(0, kernels, start_tap, 0)
    load_mask.start()
    load_target.start()
    for i in range(3, TABLES):
        loads[i].start()

    barrier = pltpu.get_barrier_semaphore()

    @pl.when(has_prev)
    def _():
        pl.semaphore_signal(barrier, inc=1, device_id=prev_id, device_id_type=MESH)

    @pl.when(has_next)
    def _():
        pl.semaphore_signal(barrier, inc=1, device_id=next_id, device_id_type=MESH)

    pl.semaphore_wait(barrier, has_prev.astype(jnp.int32) + has_next.astype(jnp.int32))

    def exchange(first, src_up, dst_up, src_down, dst_down):
        down = pltpu.make_async_remote_copy(
            src_ref=src_down,
            dst_ref=dst_down,
            send_sem=send_sem.at[first],
            recv_sem=recv_sem.at[first],
            device_id=next_id,
            device_id_type=MESH,
        )
        up = pltpu.make_async_remote_copy(
            src_ref=src_up,
            dst_ref=dst_up,
            send_sem=send_sem.at[first + 1],
            recv_sem=recv_sem.at[first + 1],
            device_id=prev_id,
            device_id_type=MESH,
        )
        return up, down

    def start_both(pair):
        up, down = pair

        @pl.when(has_next)
        def _():
            down.start()

        @pl.when(has_prev)
        def _():
            up.start()

    def wait_both(pair):
        up, down = pair

        @pl.when(has_prev)
        def _():
            up.wait_send()
            down.wait_recv()

        @pl.when(has_next)
        def _():
            down.wait_send()
            up.wait_recv()

    halo = exchange(
        0,
        mask_hbm.at[:, pl.ds(0, RMAX)],
        ext_ref.at[:, pl.ds(RMAX + rows, RMAX)],
        mask_hbm.at[:, pl.ds(rows - RMAX, RMAX)],
        ext_ref.at[:, pl.ds(0, RMAX)],
    )
    start_both(halo)

    @pl.when(jnp.logical_not(has_prev))
    def _():
        ext_ref[:, :RMAX] = jnp.zeros_like(ext_ref[:, :RMAX])
        rims[0] = jnp.zeros_like(rims[0])

    @pl.when(jnp.logical_not(has_next))
    def _():
        ext_ref[:, RMAX + rows :] = jnp.zeros_like(ext_ref[:, RMAX + rows :])
        rims[1] = jnp.zeros_like(rims[1])

    for i in range(3):
        loads[i].wait()

    def spectrum(k):
        radius = radii_ref[k]
        b = lax.broadcasted_iota(jnp.int32, (RMAX, taps), 0)
        a = lax.broadcasted_iota(jnp.int32, (RMAX, taps), 1) - RMAX
        inside = (b < radius) & (a >= -radius) & (a < radius)
        parts = []
        for part in range(2):
            turned = taps_ref[k, part].T
            parts.append(jnp.where(inside, turned[RMAX:], 0.0))
            parts.append(jnp.where(inside, flip(turned[:RMAX]), 0.0))
        quads = transform(fold_rows(*parts), tap_lane[...], tap_cos[...], tap_sin[...])
        for q, (re, im) in enumerate(quads):
            spec[k, 2 * q] = re
            spec[k, 2 * q + 1] = im

    def batch(step, carry):
        for i in range(UNROLL[0]):
            tap_load(step * UNROLL[0] + i).wait()
        for i in range(UNROLL[0]):
            spectrum(step * UNROLL[0] + i)
        return carry

    lax.fori_loop(0, kernels // UNROLL[0], batch, 0)

    load_mask.wait()
    load_target.wait()
    for i in range(3, TABLES):
        loads[i].wait()
    wait_both(halo)

    mask = jnp.concatenate([ext_ref[0].T, ext_ref[1].T], axis=0)
    half = lane_transform(mask, ext_lane[...])
    both = wide(mask_left[...], signed(half[:cols], half[cols:]))
    middle = both.shape[0] // 2
    for q, (re, im) in enumerate(quadrants(both[:middle], both[middle:])):
        acc[2 * q] = re
        acc[2 * q + 1] = im

    power_ref[...] = jnp.zeros_like(power_ref)

    def mixed(k, g):
        return jnp.where(group_ref[k] == g, weight_ref[k], 0.0)

    def forward(k, carry):
        quads = []
        for q in range(4):
            xr, xi = spec[k, 2 * q], spec[k, 2 * q + 1]
            mr, mi = acc[2 * q], acc[2 * q + 1]
            quads.append((xr * mr - xi * mi, xr * mi + xi * mr))
        field = inverse_folded(quads, back_cos[...], back_sin[...], back_own[...])
        fields[k] = field
        power = field[:cols] * field[:cols] + field[cols:] * field[cols:]
        for g in range(GROUPS):
            power_ref[g] += mixed(k, g) * power
        return carry

    lax.fori_loop(0, kernels, forward, 0, unroll=UNROLL[1])

    middle = cols // 2
    target = target_ref[...].astype(jnp.float32).T
    target = jnp.concatenate([target[middle:], flip(target[:middle])], axis=0)
    for g in range(GROUPS):
        power = power_ref[g]
        out_ref[g] = jnp.concatenate([flip(power[middle:]), power[:middle]], axis=0).T
        resist = resist_of(power)
        slopes[g] = 2.0 * (resist - target) * resist * (1.0 - resist) * STEEPNESS
    acc[...] = jnp.zeros_like(acc)

    def backward(k, carry):
        factor = (2.0 * weight_ref[k]) * slopes[group_ref[k]]
        plus, minus = factor[:middle], factor[middle:]
        parts = []
        for part in range(2):
            parts.append(plus * fields[k, part * cols : part * cols + middle])
            parts.append(minus * fields[k, part * cols + middle : (part + 1) * cols])
        quads = transform(fold_rows(*parts), own_lane[...], own_cos[...], own_sin[...])
        for q, (wr, wi) in enumerate(quads):
            xr, xi = spec[k, 2 * q], spec[k, 2 * q + 1]
            acc[2 * q] += xr * wr + xi * wi
            acc[2 * q + 1] += xr * wi - xi * wr
        return carry

    lax.fori_loop(0, kernels, backward, 0, unroll=UNROLL[2])
    quads = [(acc[2 * q], acc[2 * q + 1]) for q in range(4)]
    adjoint = inverse_wide(quads, back_left[...], back_ext[...])
    adj[0] = adjoint[:cols].T
    adj[1] = adjoint[cols:].T
    back = exchange(
        2,
        adj.at[:, pl.ds(0, RMAX)],
        rims.at[1],
        adj.at[:, pl.ds(RMAX + rows, RMAX)],
        rims.at[0],
    )
    start_both(back)
    own_ref[...] = adj[:, RMAX : RMAX + rows]
    if rows > 2 * RMAX:
        rim_ref[...] = jnp.zeros_like(rim_ref)
    wait_both(back)
    rim_ref[:, :RMAX] = rims[0]
    rim_ref[:, rows - RMAX :] = rims[1]


def finish(power_ref, own_ref, rim_ref, resist_ref, grad_ref):
    resist_ref[...] = resist_of(power_ref[...])
    grad_ref[...] = own_ref[...] + rim_ref[...]


def on_device(mask_field, target, kernel_taps, kernel_radii, kernel_group, kernel_weight):
    rows, cols = target.shape
    kernels, _, taps, _ = kernel_taps.shape
    grid_rows, grid_cols = grids(rows, cols)
    consts = [jnp.asarray(t) for t in tables(rows, cols)]
    vmem = pl.BlockSpec(memory_space=pltpu.VMEM)
    smem = pl.BlockSpec(memory_space=pltpu.SMEM)
    hbm = pl.BlockSpec(memory_space=pltpu.HBM)
    plane = (grid_cols // 2, grid_rows // 2)
    intensity, own, rim = pl.pallas_call(
        body,
        out_shape=(
            jax.ShapeDtypeStruct((GROUPS, rows, cols), jnp.float32),
            jax.ShapeDtypeStruct((2, rows, cols), jnp.float32),
            jax.ShapeDtypeStruct((2, rows, cols), jnp.float32),
        ),
        in_specs=[smem] * 3 + [hbm] * (3 + len(consts)),
        out_specs=(vmem, vmem, vmem),
        scratch_shapes=[
            pltpu.VMEM((kernels, 8) + plane, jnp.float32),
            pltpu.VMEM((kernels, 2 * cols, rows), jnp.float32),
            pltpu.VMEM((8,) + plane, jnp.float32),
            pltpu.VMEM((GROUPS, cols, rows), jnp.float32),
            pltpu.VMEM((GROUPS, cols, rows), jnp.float32),
            pltpu.VMEM(kernel_taps.shape, jnp.float32),
            pltpu.VMEM((2, rows + taps, cols), jnp.float32),
            pltpu.VMEM((rows, cols), jnp.int32),
            pltpu.VMEM((2, rows + taps, cols), jnp.float32),
            pltpu.VMEM((2, 2, RMAX, cols), jnp.float32),
        ]
        + [pltpu.VMEM(t.shape, t.dtype) for t in consts]
        + [
            pltpu.SemaphoreType.DMA((kernels,)),
            pltpu.SemaphoreType.DMA((TABLES + 2,)),
            pltpu.SemaphoreType.DMA((4,)),
            pltpu.SemaphoreType.DMA((4,)),
        ],
        compiler_params=pltpu.CompilerParams(
            vmem_limit_bytes=56 * 1024 * 1024, collective_id=0, has_side_effects=True
        ),
        name="litho",
    )(kernel_radii, kernel_group, kernel_weight, kernel_taps, mask_field, target, *consts)
    return pl.pallas_call(
        finish,
        out_shape=(
            jax.ShapeDtypeStruct((GROUPS, rows, cols), jnp.float32),
            jax.ShapeDtypeStruct((2, rows, cols), jnp.float32),
        ),
        in_specs=[vmem] * 3,
        out_specs=(vmem, vmem),
        name="finish",
    )(intensity, own, rim)


def solution(mesh):
    in_specs = (P(None, ("win", "row"), None), P(("win", "row"), None), P(), P(), P(), P())
    out_specs = (P(None, ("win", "row"), None), P(None, ("win", "row"), None))
    return jax.shard_map(
        on_device, mesh=mesh, in_specs=in_specs, out_specs=out_specs, check_vma=False
    )
```

```python
import numpy as np

import jax
import jax.numpy as jnp
from jax import lax
from jax.experimental import pallas as pl
from jax.experimental.pallas import tpu as pltpu
from jax.sharding import PartitionSpec as P

RMAX = 64
GROUPS = 3
STEEPNESS = 1.0
THRESHOLD = 2.0
UNROLL = (12, 24, 24)
TABLES = 13
MESH = pl.DeviceIdType.MESH


def split_np(table):
    high = table.astype(jnp.bfloat16)
    low = (table - high.astype(np.float64)).astype(jnp.bfloat16)
    return high, low


def angles(twice, grid):
    freqs = np.arange(grid // 2, dtype=np.int64)
    turns = (twice.astype(np.int64)[:, None] * (2 * freqs[None, :] + 1)) % (4 * grid)
    return turns.astype(np.float64) * (np.pi / (2 * grid))


def halves(count):
    return 2 * np.arange(count // 2) + 1


def grids(rows, cols):
    return rows + 2 * RMAX, cols + RMAX


def tables(rows, cols):
    taps = 2 * RMAX
    grid_rows, grid_cols = grids(rows, cols)
    tap, own = 2 * (np.arange(taps) - RMAX), 2 * (np.arange(rows) - rows // 2)
    ext = 2 * (np.arange(rows + taps) - RMAX - rows // 2)
    col = 2 * (np.arange(cols) - cols // 2)

    def right(points):
        ang = angles(points, grid_rows)
        high, low = split_np(np.concatenate([np.cos(ang), np.sin(ang)], 1))
        return np.concatenate([high, high, low, low], 0)

    def back_right(points):
        ang = angles(points, grid_rows).T
        high, low = split_np(np.concatenate([np.cos(ang), np.sin(ang)], 0) / grid_rows)
        both = np.concatenate([high, low], 1)
        return np.concatenate([both, both], 0)

    def folded(points, wave):
        high, low = split_np(wave(angles(points, grid_cols).T))
        return np.concatenate([high, high, low, low], 1)

    def back_folded(points, wave):
        high, low = split_np(wave(angles(points, grid_cols)) / grid_cols)
        return np.concatenate(
            [np.concatenate([high, high], 1), np.concatenate([low, low], 1)], 0
        )

    def left(points):
        ang = angles(points, grid_cols).T
        high, low = split_np(np.concatenate([np.cos(ang), np.sin(ang)], 0))
        return np.concatenate([high, high, low, low], 1)

    def back_left(points):
        ang = angles(points, grid_cols)
        high, low = split_np(np.concatenate([np.cos(ang), np.sin(ang)], 1) / grid_cols)
        return np.concatenate([high, high, low, low], 1)

    return (
        right(tap),
        folded(halves(taps), np.cos),
        folded(halves(taps), np.sin),
        right(ext),
        left(col),
        back_folded(halves(cols), np.cos),
        back_folded(halves(cols), np.sin),
        back_right(own),
        right(own),
        folded(halves(cols), np.cos),
        folded(halves(cols), np.sin),
        back_left(col),
        back_right(ext),
    )


def resist_of(intensity):
    return jax.nn.sigmoid(STEEPNESS * (intensity - THRESHOLD))


def dot(a, b):
    return lax.dot_general(a, b, (((1,), (0,)), ((), ())), preferred_element_type=jnp.float32)


def split(value):
    high = value.astype(jnp.bfloat16)
    low = (value - high.astype(jnp.float32)).astype(jnp.bfloat16)
    return high, low


def fold(value):
    half = value.shape[0] // 2
    return value[:half] + value[half:]


def flip(value):
    tiles = value.reshape(value.shape[0] // 8, 8, value.shape[1])
    spot = lax.broadcasted_iota(jnp.int32, tiles.shape, 1)
    for step in (4, 2, 1):
        down = pltpu.roll(tiles, step, 1)
        up = down if step == 4 else pltpu.roll(tiles, 8 - step, 1)
        tiles = down if step == 4 else jnp.where((spot & step) == 0, up, down)
    return jnp.concatenate([tiles[i] for i in range(tiles.shape[0] - 1, -1, -1)], axis=0)


def fold_rows(plus_real, minus_real, plus_imag, minus_imag):
    return jnp.concatenate(
        [
            plus_real + minus_real,
            plus_real - minus_real,
            plus_imag + minus_imag,
            plus_imag - minus_imag,
        ],
        axis=0,
    )


def lane_transform(rows, table):
    high, low = split(rows)
    return dot(jnp.concatenate([high, low, high, low], axis=1), table)


def signed(real, imag):
    width = real.shape[1] // 2
    rc, rs, ic, js = real[:, :width], real[:, width:], imag[:, :width], imag[:, width:]
    return jnp.concatenate([rc + js, ic - rs, rc - js, ic + rs], axis=1)


def unsigned(value):
    width = value.shape[1] // 4
    pr, pi, mr, mi = (value[:, i * width : (i + 1) * width] for i in range(4))
    return (
        jnp.concatenate([pr + mr, mi - pi], axis=1),
        jnp.concatenate([pi + mi, pr - mr], axis=1),
    )


def quadrants(cos_part, sin_part):
    width = cos_part.shape[1] // 4
    quads = []
    for s in range(2):
        real, imag = slice(2 * s * width, (2 * s + 1) * width), slice((2 * s + 1) * width, (2 * s + 2) * width)
        cr, ci, sr, si = cos_part[:, real], cos_part[:, imag], sin_part[:, real], sin_part[:, imag]
        quads.append((cr + si, ci - sr))
        quads.append((cr - si, ci + sr))
    return quads


def waves(quads):
    (ar, ai), (br, bi), (cr, ci), (dr, di) = quads
    cos_part = jnp.concatenate([ar + br, ai + bi, cr + dr, ci + di], axis=1)
    sin_part = jnp.concatenate([bi - ai, ar - br, di - ci, cr - dr], axis=1)
    return cos_part, sin_part


def transform(rows, lane_table, cos_table, sin_table):
    half = lane_transform(rows, lane_table)
    quarter = half.shape[0] // 4
    er, orr, ei, oi = (half[i * quarter : (i + 1) * quarter] for i in range(4))

    def along_columns(table, value):
        high, low = split(value)
        return dot(table, jnp.concatenate([high, low, high, low], axis=0))

    return quadrants(
        along_columns(cos_table, signed(er, ei)), along_columns(sin_table, signed(orr, oi))
    )


def lane_inverse(rows, table):
    high, low = split(rows)
    both = dot(jnp.concatenate([high, low], axis=1), table)
    width = both.shape[1] // 2
    return both[:, :width] + both[:, width:]


def wide(table, value):
    high, low = split(value)
    return dot(table, jnp.concatenate([high, low, high, low], axis=0))


def inverse_folded(quads, cos_table, sin_table, lane_table):
    cos_part, sin_part = waves(quads)

    def along_columns(table, value):
        high, low = split(value)
        return fold(dot(table, jnp.concatenate([high, low], axis=0)))

    er, ei = unsigned(along_columns(cos_table, cos_part))
    orr, oi = unsigned(along_columns(sin_table, sin_part))
    out = lane_inverse(jnp.concatenate([er, orr, ei, oi], axis=0), lane_table)
    quarter = out.shape[0] // 4
    er, orr, ei, oi = (out[i * quarter : (i + 1) * quarter] for i in range(4))
    return jnp.concatenate([er + orr, er - orr, ei + oi, ei - oi], axis=0)


def inverse_wide(quads, left_table, lane_table):
    cos_part, sin_part = waves(quads)
    half = wide(left_table, jnp.concatenate([cos_part, sin_part], axis=0))
    high, low = split(jnp.concatenate(unsigned(half), axis=0))
    both = dot(jnp.concatenate([high, low], axis=1), lane_table)
    width = both.shape[1] // 2
    return both[:, :width] + both[:, width:]


def body(
    radii_ref,
    group_ref,
    weight_ref,
    taps_hbm,
    mask_hbm,
    target_hbm,
    *refs,
):
    table_hbm, refs = refs[:TABLES], refs[TABLES:]
    out_ref, own_ref, rim_ref = refs[:3]
    spec, fields, acc, power_ref, slopes, taps_ref, ext_ref, target_ref, adj, rims = refs[3:13]
    table_ref, refs = refs[13 : 13 + TABLES], refs[13 + TABLES :]
    tap_sem, load_sem, send_sem, recv_sem = refs
    tap_lane, tap_cos, tap_sin, ext_lane, mask_left = table_ref[:5]
    back_cos, back_sin, back_own, own_lane, own_cos, own_sin = table_ref[5:11]
    back_left, back_ext = table_ref[11:]
    kernels, _, taps, _ = taps_hbm.shape
    rows, cols = target_hbm.shape
    me, count = lax.axis_index("row"), lax.axis_size("row")
    has_prev, has_next = me > 0, me < count - 1
    prev_id = {"row": lax.rem(me + count - 1, count)}
    next_id = {"row": lax.rem(me + 1, count)}

    def load(src, dst, slot):
        return pltpu.make_async_copy(src, dst, load_sem.at[slot])

    def tap_load(k):
        return pltpu.make_async_copy(taps_hbm.at[k], taps_ref.at[k], tap_sem.at[k])

    loads = [load(src, dst, i) for i, (src, dst) in enumerate(zip(table_hbm, table_ref))]
    load_mask = load(mask_hbm, ext_ref.at[:, pl.ds(RMAX, rows)], TABLES)
    load_target = load(target_hbm, target_ref, TABLES + 1)
    for i in range(3):
        loads[i].start()

    def start_tap(k, carry):
        tap_load(k).start()
        return carry

    lax.fori_loop(0, kernels, start_tap, 0)
    load_mask.start()
    load_target.start()
    for i in range(3, TABLES):
        loads[i].start()

    barrier = pltpu.get_barrier_semaphore()

    @pl.when(has_prev)
    def _():
        pl.semaphore_signal(barrier, inc=1, device_id=prev_id, device_id_type=MESH)

    @pl.when(has_next)
    def _():
        pl.semaphore_signal(barrier, inc=1, device_id=next_id, device_id_type=MESH)

    def exchange(first, src_up, dst_up, src_down, dst_down):
        down = pltpu.make_async_remote_copy(
            src_ref=src_down,
            dst_ref=dst_down,
            send_sem=send_sem.at[first],
            recv_sem=recv_sem.at[first],
            device_id=next_id,
            device_id_type=MESH,
        )
        up = pltpu.make_async_remote_copy(
            src_ref=src_up,
            dst_ref=dst_up,
            send_sem=send_sem.at[first + 1],
            recv_sem=recv_sem.at[first + 1],
            device_id=prev_id,
            device_id_type=MESH,
        )
        return up, down

    def start_both(pair):
        up, down = pair

        @pl.when(has_next)
        def _():
            down.start()

        @pl.when(has_prev)
        def _():
            up.start()

    def wait_both(pair):
        up, down = pair

        @pl.when(has_prev)
        def _():
            up.wait_send()
            down.wait_recv()

        @pl.when(has_next)
        def _():
            down.wait_send()
            up.wait_recv()

    halo = exchange(
        0,
        mask_hbm.at[:, pl.ds(0, RMAX)],
        ext_ref.at[:, pl.ds(RMAX + rows, RMAX)],
        mask_hbm.at[:, pl.ds(rows - RMAX, RMAX)],
        ext_ref.at[:, pl.ds(0, RMAX)],
    )
    @pl.when(jnp.logical_not(has_prev))
    def _():
        ext_ref[:, :RMAX] = jnp.zeros_like(ext_ref[:, :RMAX])
        rims[0] = jnp.zeros_like(rims[0])

    @pl.when(jnp.logical_not(has_next))
    def _():
        ext_ref[:, RMAX + rows :] = jnp.zeros_like(ext_ref[:, RMAX + rows :])
        rims[1] = jnp.zeros_like(rims[1])

    for i in range(3):
        loads[i].wait()

    def spectrum(k):
        radius = radii_ref[k]
        b = lax.broadcasted_iota(jnp.int32, (RMAX, taps), 0)
        a = lax.broadcasted_iota(jnp.int32, (RMAX, taps), 1) - RMAX
        inside = (b < radius) & (a >= -radius) & (a < radius)
        parts = []
        for part in range(2):
            turned = taps_ref[k, part].T
            parts.append(jnp.where(inside, turned[RMAX:], 0.0))
            parts.append(jnp.where(inside, flip(turned[:RMAX]), 0.0))
        quads = transform(fold_rows(*parts), tap_lane[...], tap_cos[...], tap_sin[...])
        for q, (re, im) in enumerate(quads):
            spec[k, 2 * q] = re
            spec[k, 2 * q + 1] = im

    def batch(step, carry):
        for i in range(UNROLL[0]):
            tap_load(step * UNROLL[0] + i).wait()
        for i in range(UNROLL[0]):
            spectrum(step * UNROLL[0] + i)
        return carry

    lax.fori_loop(0, 1, batch, 0)
    pl.semaphore_wait(barrier, has_prev.astype(jnp.int32) + has_next.astype(jnp.int32))
    start_both(halo)
    lax.fori_loop(1, kernels // UNROLL[0], batch, 0)

    load_mask.wait()
    load_target.wait()
    for i in range(3, TABLES):
        loads[i].wait()
    wait_both(halo)

    mask = jnp.concatenate([ext_ref[0].T, ext_ref[1].T], axis=0)
    half = lane_transform(mask, ext_lane[...])
    both = wide(mask_left[...], signed(half[:cols], half[cols:]))
    middle = both.shape[0] // 2
    for q, (re, im) in enumerate(quadrants(both[:middle], both[middle:])):
        acc[2 * q] = re
        acc[2 * q + 1] = im

    power_ref[...] = jnp.zeros_like(power_ref)

    def mixed(k, g):
        return jnp.where(group_ref[k] == g, weight_ref[k], 0.0)

    def forward(k, carry):
        quads = []
        for q in range(4):
            xr, xi = spec[k, 2 * q], spec[k, 2 * q + 1]
            mr, mi = acc[2 * q], acc[2 * q + 1]
            quads.append((xr * mr - xi * mi, xr * mi + xi * mr))
        field = inverse_folded(quads, back_cos[...], back_sin[...], back_own[...])
        fields[k] = field
        power = field[:cols] * field[:cols] + field[cols:] * field[cols:]
        for g in range(GROUPS):
            power_ref[g] += mixed(k, g) * power
        return carry

    lax.fori_loop(0, kernels, forward, 0, unroll=UNROLL[1])

    middle = cols // 2
    target = target_ref[...].astype(jnp.float32).T
    target = jnp.concatenate([target[middle:], flip(target[:middle])], axis=0)
    for g in range(GROUPS):
        power = power_ref[g]
        out_ref[g] = jnp.concatenate([flip(power[middle:]), power[:middle]], axis=0).T
        resist = resist_of(power)
        slopes[g] = 2.0 * (resist - target) * resist * (1.0 - resist) * STEEPNESS
    acc[...] = jnp.zeros_like(acc)

    def backward(k, carry):
        factor = (2.0 * weight_ref[k]) * slopes[group_ref[k]]
        plus, minus = factor[:middle], factor[middle:]
        parts = []
        for part in range(2):
            parts.append(plus * fields[k, part * cols : part * cols + middle])
            parts.append(minus * fields[k, part * cols + middle : (part + 1) * cols])
        quads = transform(fold_rows(*parts), own_lane[...], own_cos[...], own_sin[...])
        for q, (wr, wi) in enumerate(quads):
            xr, xi = spec[k, 2 * q], spec[k, 2 * q + 1]
            acc[2 * q] += xr * wr + xi * wi
            acc[2 * q + 1] += xr * wi - xi * wr
        return carry

    lax.fori_loop(0, kernels, backward, 0, unroll=UNROLL[2])
    quads = [(acc[2 * q], acc[2 * q + 1]) for q in range(4)]
    adjoint = inverse_wide(quads, back_left[...], back_ext[...])
    adj[0] = adjoint[:cols].T
    adj[1] = adjoint[cols:].T
    back = exchange(
        2,
        adj.at[:, pl.ds(0, RMAX)],
        rims.at[1],
        adj.at[:, pl.ds(RMAX + rows, RMAX)],
        rims.at[0],
    )
    start_both(back)
    own_ref[...] = adj[:, RMAX : RMAX + rows]
    if rows > 2 * RMAX:
        rim_ref[...] = jnp.zeros_like(rim_ref)
    wait_both(back)
    rim_ref[:, :RMAX] = rims[0]
    rim_ref[:, rows - RMAX :] = rims[1]


def finish(power_ref, own_ref, rim_ref, resist_ref, grad_ref):
    resist_ref[...] = resist_of(power_ref[...])
    grad_ref[...] = own_ref[...] + rim_ref[...]


def on_device(mask_field, target, kernel_taps, kernel_radii, kernel_group, kernel_weight):
    rows, cols = target.shape
    kernels, _, taps, _ = kernel_taps.shape
    grid_rows, grid_cols = grids(rows, cols)
    consts = [jnp.asarray(t) for t in tables(rows, cols)]
    vmem = pl.BlockSpec(memory_space=pltpu.VMEM)
    smem = pl.BlockSpec(memory_space=pltpu.SMEM)
    hbm = pl.BlockSpec(memory_space=pltpu.HBM)
    plane = (grid_cols // 2, grid_rows // 2)
    intensity, own, rim = pl.pallas_call(
        body,
        out_shape=(
            jax.ShapeDtypeStruct((GROUPS, rows, cols), jnp.float32),
            jax.ShapeDtypeStruct((2, rows, cols), jnp.float32),
            jax.ShapeDtypeStruct((2, rows, cols), jnp.float32),
        ),
        in_specs=[smem] * 3 + [hbm] * (3 + len(consts)),
        out_specs=(vmem, vmem, vmem),
        scratch_shapes=[
            pltpu.VMEM((kernels, 8) + plane, jnp.float32),
            pltpu.VMEM((kernels, 2 * cols, rows), jnp.float32),
            pltpu.VMEM((8,) + plane, jnp.float32),
            pltpu.VMEM((GROUPS, cols, rows), jnp.float32),
            pltpu.VMEM((GROUPS, cols, rows), jnp.float32),
            pltpu.VMEM(kernel_taps.shape, jnp.float32),
            pltpu.VMEM((2, rows + taps, cols), jnp.float32),
            pltpu.VMEM((rows, cols), jnp.int32),
            pltpu.VMEM((2, rows + taps, cols), jnp.float32),
            pltpu.VMEM((2, 2, RMAX, cols), jnp.float32),
        ]
        + [pltpu.VMEM(t.shape, t.dtype) for t in consts]
        + [
            pltpu.SemaphoreType.DMA((kernels,)),
            pltpu.SemaphoreType.DMA((TABLES + 2,)),
            pltpu.SemaphoreType.DMA((4,)),
            pltpu.SemaphoreType.DMA((4,)),
        ],
        compiler_params=pltpu.CompilerParams(
            vmem_limit_bytes=56 * 1024 * 1024, collective_id=0, has_side_effects=True
        ),
        name="litho",
    )(kernel_radii, kernel_group, kernel_weight, kernel_taps, mask_field, target, *consts)
    return pl.pallas_call(
        finish,
        out_shape=(
            jax.ShapeDtypeStruct((GROUPS, rows, cols), jnp.float32),
            jax.ShapeDtypeStruct((2, rows, cols), jnp.float32),
        ),
        in_specs=[vmem] * 3,
        out_specs=(vmem, vmem),
        name="finish",
    )(intensity, own, rim)


def solution(mesh):
    in_specs = (P(None, ("win", "row"), None), P(("win", "row"), None), P(), P(), P(), P())
    out_specs = (P(None, ("win", "row"), None), P(None, ("win", "row"), None))
    return jax.shard_map(
        on_device, mesh=mesh, in_specs=in_specs, out_specs=out_specs, check_vma=False
    )
```
